32 devices in a mesh: comp: 4 (over x, core), mom: 8 (over z, y).
Axes of the slice: x: 2, y: 2, z: 4, core: 2. Of those that a mesh axis runs over, the one named last changes fastest.
Arguments:
- green_guess: float32 [4, 512, 192, 384], P('comp', 'mom'), may hold values from -3 to 3
- green_free: float32 [4, 512, 192, 384], P('comp', 'mom'), may hold values from -3 to 3
- retarded: float32 [512, 192, 384], P('mom'), may hold values from -0.3125 to 0.3125
- momentum_order: int32 [512], replicated, may hold values from 0 to 511, each once
Outputs:
- green_final: float32 [4, 512, 192, 384], P('comp', 'mom')
- self_energy: float32 [4, 512, 192, 384], P('comp', 'mom')
The draws below stay inside these ranges and needn't reach their ends.
Inputs may be any that keep to these rules, and one draw needn't show every extreme that they name: `momentum_order`: a permutation of the lattice momenta 0 to 511.
All inputs are finite; a program needn't handle non-finite values.
Results may differ from the reference program's by a relative error of at most 0.00013.
Values sent between devices are 32-bit elements; how exact they have to be, the bound alone decides.
A program may use at most 192 MiB of HBM per device.

```python
import math
import jax
import jax.numpy as jnp
from jax import lax

COMP = 4
K = 512
L1 = 16
NT = 192
ITERS = 1


def block_levels(rng, extent, cuts, least, top_value):
    def one(position, shards_of):
        steps = jax.random.uniform(jax.random.fold_in(jax.random.fold_in(rng, 6), position), (shards_of,), jnp.float32, least / len(cuts), top_value / len(cuts))
        return jnp.repeat(jnp.exp(steps), extent[position] // shards_of).reshape((-1,) + (1,) * (len(extent) - position - 1))

    level = one(*cuts[0])
    for cut in cuts[1:]:
        level = level * one(*cut)
    return level


def scatter_about(stream_key, shape, spread, bound, shards=(), kind=jnp.bfloat16):
    factor_of = block_levels(stream_key, shape, shards, -0.22, 0.18) if shards else 1.0
    result = jax.random.normal(stream_key, shape, jnp.float32) * spread * factor_of
    return jnp.minimum(jnp.maximum(result, -bound), bound).astype(kind)


def setup_inputs(seed: int = 0) -> dict:
    key_list = jax.random.split(jax.random.key(seed), 5)
    return {
        "green_guess": scatter_about(key_list[0], (COMP, K, NT, 2 * NT), 0.5, 3.0, ((0, 4), (1, 8)), jnp.float32),
        "green_free": scatter_about(key_list[1], (COMP, K, NT, 2 * NT), 0.5, 3.0, ((0, 4), (1, 8)), jnp.float32),
        "retarded": scatter_about(key_list[2], (K, NT, 2 * NT), (2 * NT) ** -0.5, 0.3125, ((0, 8),), jnp.float32),
        "momentum_order": jax.random.permutation(key_list[3], K).astype(jnp.int32),
    }


highest = lax.Precision.HIGHEST

def phase_tables(momentum_order, count, first_len):
    second_len = count // first_len
    site_ids = jnp.arange(count, dtype=jnp.int32)
    site_one = site_ids // second_len
    site_two = site_ids % second_len
    mom_one = momentum_order.astype(jnp.int32) // second_len
    mom_two = momentum_order.astype(jnp.int32) % second_len
    phases = (site_one[:, None] * mom_one[None, :] * second_len + site_two[:, None] * mom_two[None, :] * first_len) % count
    angles = phases.astype(jnp.float32) * (2.0 * math.pi / count)
    norm_factor = 1.0 / math.sqrt(count)
    return (jnp.cos(angles) * norm_factor, jnp.sin(angles) * norm_factor)

def forward_transform(values, cosine, sine_table, half_width):
    full_shape = values.shape
    flattened = values.reshape(full_shape[0], -1)
    with_cos = jnp.dot(cosine, flattened, precision=highest, preferred_element_type=jnp.float32).reshape(full_shape)
    with_sin = jnp.dot(sine_table, flattened, precision=highest, preferred_element_type=jnp.float32).reshape(full_shape)
    real_part = with_cos[..., :half_width] - with_sin[..., half_width:]
    imag_part = with_cos[..., half_width:] + with_sin[..., :half_width]
    return jnp.concatenate([real_part, imag_part], axis=-1)

def inverse_transform(values, cos_back, sin_back, half_width):
    full_shape = values.shape
    flattened = values.reshape(full_shape[0], -1)
    with_cos = jnp.dot(cos_back, flattened, precision=highest, preferred_element_type=jnp.float32).reshape(full_shape)
    with_sin = jnp.dot(sin_back, flattened, precision=highest, preferred_element_type=jnp.float32).reshape(full_shape)
    real_part = with_cos[..., :half_width] + with_sin[..., half_width:]
    imag_part = with_cos[..., half_width:] - with_sin[..., :half_width]
    return jnp.concatenate([real_part, imag_part], axis=-1)

def triple(own_part, second, conj_factor, half_width):
    prod_real = own_part[..., :half_width] * second[..., :half_width] - own_part[..., half_width:] * second[..., half_width:]
    prod_imag = own_part[..., :half_width] * second[..., half_width:] + own_part[..., half_width:] * second[..., :half_width]
    conj_real = conj_factor[..., :half_width]
    conj_imag = conj_factor[..., half_width:]
    real_part = prod_real * conj_real + prod_imag * conj_imag
    imag_part = prod_imag * conj_real - prod_real * conj_imag
    return -jnp.concatenate([real_part, imag_part], axis=-1)

def dyson(sigma_mom, retarded, free_part, half_width):
    ret_real = retarded[..., :half_width]
    ret_imag = retarded[..., half_width:]
    swapped = jnp.concatenate([-sigma_mom[..., half_width:], sigma_mom[..., :half_width]], axis=-1)
    left_prod = jnp.einsum('kij,kjx->kix', ret_real, sigma_mom, precision=highest, preferred_element_type=jnp.float32)
    left_prod = left_prod + jnp.einsum('kij,kjx->kix', ret_imag, swapped, precision=highest, preferred_element_type=jnp.float32)
    turned = jnp.concatenate([left_prod[..., half_width:], -left_prod[..., :half_width]], axis=-1)
    real_part = jnp.einsum('kim,kjm->kij', left_prod, retarded, precision=highest, preferred_element_type=jnp.float32)
    imag_part = jnp.einsum('kim,kjm->kij', turned, retarded, precision=highest, preferred_element_type=jnp.float32)
    return free_part + jnp.concatenate([real_part, imag_part], axis=-1)

def reference(green_guess, green_free, retarded, momentum_order):
    half_width = NT
    row_block = 8
    cosine, sine_table = phase_tables(momentum_order, K, L1)
    cos_back = cosine.T
    sin_back = sine_table.T
    free_by_mom = jnp.moveaxis(green_free, 1, 0)
    current = green_guess
    sigma_out = green_guess

    def one_block(row_piece):
        by_moment = jnp.moveaxis(row_piece, 1, 0)
        in_sites = forward_transform(by_moment, cosine, sine_table, half_width)
        second = jnp.concatenate([in_sites[:, 2:], in_sites[:, :2]], axis=1)
        conj_factor = jnp.flip(in_sites, axis=1)
        sigma_sites = triple(in_sites, second, conj_factor, half_width)
        return inverse_transform(sigma_sites, cos_back, sin_back, half_width)

    def one_moment(inputs_k):
        sigma_k, ret_k, free_k = inputs_k
        ret_many = jnp.broadcast_to(ret_k[None], (COMP, NT, 2 * NT))
        return dyson(sigma_k, ret_many, free_k, half_width)
    for iteration in range(ITERS):
        blocks = current.reshape(COMP, K, NT // row_block, row_block, 2 * NT)
        blocks = jnp.moveaxis(blocks, 2, 0)
        sigma_blocks = lax.map(one_block, blocks)
        sigma_mom = jnp.transpose(sigma_blocks, (1, 2, 0, 3, 4)).reshape(K, COMP, NT, 2 * NT)
        updated = lax.map(one_moment, (sigma_mom, retarded, free_by_mom))
        current = jnp.moveaxis(updated, 0, 1)
        sigma_out = jnp.moveaxis(sigma_mom, 0, 1)
    return (current, sigma_out)
```

```python
import functools
import math

import jax
import jax.numpy as jnp
from jax import lax
from jax.experimental import pallas as pl
from jax.experimental.pallas import tpu as pltpu
from jax.sharding import PartitionSpec as P

K = 512
L1 = 16


highest = lax.Precision.HIGH


def partner(x, axis, bit):
    return lax.ppermute(x, axis, [(i, i ^ 1 << bit) for i in range(lax.axis_size(axis))])


def phase_tables(momentum_order, count, first_len):
    second_len = count // first_len
    site_ids = jnp.arange(count, dtype=jnp.int32)
    site_one = site_ids // second_len
    site_two = site_ids % second_len
    mom_one = momentum_order // second_len
    mom_two = momentum_order % second_len
    phases = (
        site_one[:, None] * mom_one[None, :] * second_len
        + site_two[:, None] * mom_two[None, :] * first_len
    ) % count
    angles = phases.astype(jnp.float32) * (2.0 * math.pi / count)
    norm_factor = 1.0 / math.sqrt(count)
    return (jnp.cos(angles) * norm_factor, jnp.sin(angles) * norm_factor)


def forward_transform(values, cosine, sine_table, half_width):
    full_shape = values.shape
    flattened = values.reshape(full_shape[0], -1)
    with_cos = jnp.dot(
        cosine, flattened, precision=highest, preferred_element_type=jnp.float32
    ).reshape(full_shape)
    with_sin = jnp.dot(
        sine_table, flattened, precision=highest, preferred_element_type=jnp.float32
    ).reshape(full_shape)
    real_part = with_cos[..., :half_width] - with_sin[..., half_width:]
    imag_part = with_cos[..., half_width:] + with_sin[..., :half_width]
    return jnp.concatenate([real_part, imag_part], axis=-1)


def inverse_transform(values, cos_back, sin_back, half_width):
    full_shape = values.shape
    flattened = values.reshape(full_shape[0], -1)
    with_cos = jnp.dot(
        cos_back, flattened, precision=highest, preferred_element_type=jnp.float32
    ).reshape(full_shape)
    with_sin = jnp.dot(
        sin_back, flattened, precision=highest, preferred_element_type=jnp.float32
    ).reshape(full_shape)
    real_part = with_cos[..., :half_width] + with_sin[..., half_width:]
    imag_part = with_cos[..., half_width:] - with_sin[..., :half_width]
    return jnp.concatenate([real_part, imag_part], axis=-1)


def triple(own_part, second, conj_factor, half_width):
    prod_real = (
        own_part[..., :half_width] * second[..., :half_width]
        - own_part[..., half_width:] * second[..., half_width:]
    )
    prod_imag = (
        own_part[..., :half_width] * second[..., half_width:]
        + own_part[..., half_width:] * second[..., :half_width]
    )
    conj_real = conj_factor[..., :half_width]
    conj_imag = conj_factor[..., half_width:]
    real_part = prod_real * conj_real + prod_imag * conj_imag
    imag_part = prod_imag * conj_real - prod_real * conj_imag
    return -jnp.concatenate([real_part, imag_part], axis=-1)


def dyson(sigma_mom, retarded, free_part, half_width):
    ret_real = retarded[..., :half_width]
    ret_imag = retarded[..., half_width:]
    swapped = jnp.concatenate([-sigma_mom[..., half_width:], sigma_mom[..., :half_width]], axis=-1)
    left_prod = jnp.einsum(
        "kij,kjx->kix", ret_real, sigma_mom, precision=highest, preferred_element_type=jnp.float32
    )
    left_prod = left_prod + jnp.einsum(
        "kij,kjx->kix", ret_imag, swapped, precision=highest, preferred_element_type=jnp.float32
    )
    turned = jnp.concatenate([left_prod[..., half_width:], -left_prod[..., :half_width]], axis=-1)
    real_part = jnp.einsum(
        "kim,kjm->kij", left_prod, retarded, precision=highest, preferred_element_type=jnp.float32
    )
    imag_part = jnp.einsum(
        "kim,kjm->kij", turned, retarded, precision=highest, preferred_element_type=jnp.float32
    )
    return free_part + jnp.concatenate([real_part, imag_part], axis=-1)


CHUNKS = 3
GROUPS = 4


def exchange(send, axis):
    size = lax.axis_size(axis)
    return [send[0]] + [
        lax.ppermute(send[s], axis, [(i, i ^ s) for i in range(size)]) for s in range(1, size)
    ]


def on_device_plain(green_guess, green_free, retarded, momentum_order):
    mom_count = lax.axis_size("mom")
    me = lax.axis_index("mom")
    width = green_guess.shape[-1]
    half_width = width // 2
    k_local = green_guess.shape[1]
    tile_rows = half_width // mom_count
    rows = tile_rows // CHUNKS
    group = k_local // GROUPS
    cosine, sine_table = phase_tables(momentum_order, K, L1)
    cos_back = cosine.T
    sin_back = sine_table.T
    free_local = green_free[0]
    current = green_guess[0]

    tiled = current.reshape(k_local, mom_count, CHUNKS, rows, width)
    arrived = [
        lax.all_to_all(tiled[:, :, c], "mom", split_axis=1, concat_axis=0, tiled=True)
        for c in range(CHUNKS)
    ]
    pieces = []
    for c in range(CHUNKS):
        in_sites = forward_transform(arrived[c][:, 0], cosine, sine_table, half_width)
        spin_other = partner(in_sites, "comp", 1)
        cross_other = partner(spin_other, "comp", 0)
        sigma_sites = triple(in_sites, spin_other, cross_other, half_width)
        tile = inverse_transform(sigma_sites, cos_back, sin_back, half_width)
        pieces.append(lax.all_to_all(tile.reshape(mom_count, k_local, 1, rows, width), "mom", split_axis=0, concat_axis=2, tiled=True))
    sigma = jnp.stack(pieces, axis=3).reshape(k_local, half_width, width)
    return (dyson(sigma, retarded, free_local, half_width)[None], sigma[None])


BF16 = jnp.bfloat16
F32 = jnp.float32
SUBLANES = 8
LANES = 128
GROUP_COUNT = 4
MESH = pl.DeviceIdType.MESH


def flip(index, mask, count):
    out, bit = 0, 1
    while bit < count:
        part = lax.rem(lax.div(index, bit), 2)
        out = out + bit * ((1 - part) if (mask // bit) % 2 else part)
        bit *= 2
    return out


def split(value):
    high = value.astype(BF16)
    return high, (value - high.astype(F32)).astype(BF16)


def mm(left, right, dims=((1,), (0,))):
    return lax.dot_general(left, right, (dims, ((), ())), preferred_element_type=F32)


def mm3(left, right, dims=((1,), (0,))):
    return mm(left[0], right[0], dims) + (mm(left[0], right[1], dims) + mm(left[1], right[0], dims))


def small_tables(momentum_order, count, first_len):
    second_len = count // first_len
    ids = jnp.arange(first_len + second_len, dtype=jnp.int32)[:, None]
    mom_one = (momentum_order // second_len)[None, :]
    mom_two = (momentum_order % second_len)[None, :]
    phases = jnp.where(
        ids < first_len,
        (ids * mom_one * second_len) % count,
        ((ids - first_len) * mom_two * first_len) % count,
    )
    angles = phases.astype(F32) * (2.0 * math.pi / count)
    scale = jnp.where(ids < first_len, 1.0 / math.sqrt(count), 1.0).astype(F32)
    return jnp.cos(angles) * scale, jnp.sin(angles) * scale


def dyson_block(sigma, ret, free, half):
    width = 2 * half
    lane = lax.broadcasted_iota(jnp.int32, sigma.shape, 1)
    sign = jnp.where(lane < half, -1.0, 1.0).astype(F32)
    sig_pair = [jnp.concatenate(p, axis=0) for p in zip(split(sigma), split(pltpu.roll(sigma, half, 1) * sign))]
    ret_parts = split(ret)
    ret_pair = [jnp.concatenate(p, axis=0) for p in zip(ret_parts, split(pltpu.roll(ret, half, 1) * sign))]
    left = mm3(ret_parts, sig_pair)
    return free + mm3(split(left), ret_pair, ((1,), (1,)))


def dyson_kernel(half, sig_ref, ret_ref, free_ref, green_ref, out_ref):
    sigma = sig_ref[0]
    out_ref[0] = sigma
    green_ref[0] = dyson_block(sigma, ret_ref[0], free_ref[0], half)


def dyson_call(sigma, retarded, free):
    count, half, width = sigma.shape
    spec = pl.BlockSpec((1, half, width), lambda k: (k, 0, 0))
    shape = jax.ShapeDtypeStruct(sigma.shape, F32)
    return pl.pallas_call(
        functools.partial(dyson_kernel, half),
        grid=(count,),
        in_specs=[spec] * 3,
        out_specs=(spec, spec),
        out_shape=(shape, shape),
        name="dyson",
    )(sigma, retarded, free)


def born_kernel(
    n, chunks, first_len,
    x_hbm, cos_ref, sin_ref,
    recv_hbm, sig_hbm,
    buf, site, gs, qsend, q, zhi, zlo, fwd_hi, fwd_lo, inv_hi, inv_lo,
    fwd_send, fwd_recv, load_sem, gs_send, gs_recv, q_send, q_recv, rel_send, rel_recv, ret_send, ret_recv, own_sem, stage_sem,
):
    me = lax.axis_index("mom")
    comp = lax.axis_index("comp")
    core = lax.rem(comp, 2)
    sibling = {"comp": comp + 1 - 2 * core}
    across = {"comp": lax.rem(comp + 2, 4)}
    sgn = (1 - 2 * core).astype(F32)
    k_local, full, width = x_hbm.shape
    half = width // 2
    count = n * k_local
    rows = SUBLANES
    pairs = rows // 2
    cols = pairs * width
    second_len = count // first_len
    group = k_local // GROUP_COUNT
    masks = list(range(n // 2, n)) + list(range(1, n // 2))
    peers = [flip(me, s, n) for s in masks]
    hr = count // 2

    barrier = pltpu.get_barrier_semaphore()
    for peer in peers:
        pl.semaphore_signal(barrier, inc=1, device_id={"mom": peer}, device_id_type=MESH)
    pl.semaphore_signal(barrier, inc=1, device_id=sibling, device_id_type=MESH)
    pl.semaphore_signal(barrier, inc=1, device_id=across, device_id_type=MESH)
    pl.semaphore_wait(barrier, len(peers) + 2)

    def row_of(device, c):
        return pl.multiple_of((device * chunks + c) * rows, rows)

    def fwd_copy(c, i):
        return pltpu.make_async_remote_copy(
            src_ref=x_hbm.at[:, pl.ds(row_of(peers[i], c), rows), :],
            dst_ref=recv_hbm.at[c, pl.ds(me * k_local, k_local)],
            send_sem=fwd_send.at[c, i], recv_sem=fwd_recv.at[c, i],
            device_id={"mom": peers[i]}, device_id_type=MESH)

    def ret_copy(c, g, i):
        return pltpu.make_async_remote_copy(
            src_ref=recv_hbm.at[c, pl.ds(peers[i] * k_local + g * group, group)],
            dst_ref=sig_hbm.at[pl.ds(g * group, group), pl.ds(row_of(me, c), rows), :],
            send_sem=ret_send.at[c, g, i], recv_sem=ret_recv.at[c, g, i],
            device_id={"mom": peers[i]}, device_id_type=MESH)

    def send_forward(c, carry):
        for i in range(len(peers)):
            fwd_copy(c, i).start()
        return carry

    lax.fori_loop(0, chunks, send_forward, 0)

    def build(one, carry):
        c1 = cos_ref[pl.ds(one, 1), :]
        s1 = sin_ref[pl.ds(one, 1), :]
        c2 = cos_ref[pl.ds(first_len, second_len), :]
        s2 = sin_ref[pl.ds(first_len, second_len), :]
        at = pl.ds(pl.multiple_of(one * second_len, second_len), second_len)
        low = pl.ds(pl.multiple_of(count + one * second_len, second_len), second_len)
        cosine = c1 * c2 - s1 * s2
        sine = s1 * c2 + c1 * s2
        site[0, at, 0:count] = cosine
        site[1, at, 0:count] = sine
        ch, cl = split(cosine)
        sh, sl = split(sine)
        for ref, cv, sv in ((fwd_hi, ch, sh), (fwd_lo, cl, sl)):
            ref[at, 0:count] = cv
            ref[at, count:2 * count] = -sv
            ref[low, 0:count] = sv
            ref[low, count:2 * count] = cv
        return carry

    lax.fori_loop(0, first_len, build, 0)

    def turn(b, carry):
        at = pl.ds(pl.multiple_of(b * 128, 128), 128)
        low = pl.ds(pl.multiple_of(count + b * 128, 128), 128)
        ch, cl = split(site[0, :, at].T)
        sh, sl = split(site[1, :, at].T)
        for ref, cv, sv in ((inv_hi, ch, sh), (inv_lo, cl, sl)):
            ref[at, 0:count] = cv
            ref[at, count:2 * count] = sv
            ref[low, 0:count] = -sv
            ref[low, count:2 * count] = cv
        return carry

    lax.fori_loop(0, count // 128, turn, 0)

    tiles = width // LANES
    flat = buf.reshape(tiles, count * rows, LANES)

    def take(start, size):
        return jnp.concatenate([flat[j, pl.ds(start, size, stride=rows), :] for j in range(tiles)], axis=1)

    def put(start, size, value):
        for j in range(tiles):
            flat[j, pl.ds(start, size, stride=rows), :] = value[:, j * LANES:(j + 1) * LANES]

    def lanes_of(j):
        return pl.ds(j * LANES, LANES)


    def chunk_step(c, carry):
        slot = lax.rem(c, 2)
        loads = []
        for j in range(tiles):
            loads.append(pltpu.make_async_copy(
                x_hbm.at[:, pl.ds(row_of(me, c), rows), lanes_of(j)],
                buf.at[j, pl.ds(me * k_local, k_local)], load_sem.at[n - 1, j]))
            loads[-1].start()
        for i in range(len(peers)):
            fwd_copy(c, i).wait_recv()
            at = pl.ds(peers[i] * k_local, k_local)
            for j in range(tiles):
                loads.append(pltpu.make_async_copy(
                    recv_hbm.at[c, at, :, lanes_of(j)], buf.at[j, at], load_sem.at[i, j]))
                loads[-1].start()
        for load in loads:
            load.wait()

        kb = k_local

        def stage(b, carry):
            lane = lax.broadcasted_iota(jnp.int32, (kb, width), 1)
            at = pl.ds(pl.multiple_of(b * kb, kb), kb)
            low = pl.ds(pl.multiple_of(count + b * kb, kb), kb)
            for p in range(pairs):
                r0 = take(b * (kb * rows) + 2 * p, kb)
                r1 = take(b * (kb * rows) + 2 * p + 1, kb)
                re = jnp.where(lane < half, r0, pltpu.roll(r1, half, 1))
                im = jnp.where(lane < half, pltpu.roll(r0, half, 1), r1)
                here = pl.ds(p * width, width)
                rh, rl = split(re)
                ih, il = split(im)
                zhi[at, here] = rh
                zlo[at, here] = rl
                zhi[low, here] = ih
                zlo[low, here] = il
            return carry

        lax.fori_loop(0, count // kb, stage, 0)

        def forward(step, carry):
            m, t = lax.div(step, 3), lax.rem(step, 3)
            plane, part = lax.div(m, 2), lax.rem(m, 2)
            left = pl.ds(pl.multiple_of(m * hr, hr), hr)
            right = pl.ds(pl.multiple_of(t * (cols // 3), cols // 3), cols // 3)
            value = mm3((fwd_hi[left, :], fwd_lo[left, :]), (zhi[:, right], zlo[:, right]))
            site[plane, pl.ds(pl.multiple_of(part * hr, hr), hr), right] = value
            return carry

        lax.fori_loop(0, 12, forward, 0)

        mine = pl.multiple_of(core * hr, hr)
        other = pl.multiple_of((1 - core) * hr, hr)
        gs_copy = pltpu.make_async_remote_copy(
            src_ref=site.at[:, pl.ds(other, hr), :], dst_ref=gs.at[slot],
            send_sem=gs_send, recv_sem=gs_recv.at[slot], device_id=sibling, device_id_type=MESH)
        gs_copy.start()
        gs_copy.wait_recv()

        rb = 16

        def pair(b, carry):
            here = pl.ds(pl.multiple_of(b * rb, rb), rb)
            at = pl.ds(pl.multiple_of(mine + b * rb, rb), rb)
            ore, oim = site[0, at, :], site[1, at, :]
            sre, sim = gs[slot, 0, here, :], gs[slot, 1, here, :]
            qsend[0, here, :] = ore * sre + oim * sim
            qsend[1, here, :] = sgn * (oim * sre - ore * sim)
            return carry

        lax.fori_loop(0, hr // rb, pair, 0)

        q_copy = pltpu.make_async_remote_copy(
            src_ref=qsend, dst_ref=q.at[slot, :, pl.ds(mine, hr), :],
            send_sem=q_send, recv_sem=q_recv.at[slot], device_id=across, device_id_type=MESH)
        q_copy.start()
        q_copy.wait_recv()
        relay = pltpu.make_async_remote_copy(
            src_ref=q.at[slot, :, pl.ds(mine, hr), :], dst_ref=q.at[slot, :, pl.ds(mine, hr), :],
            send_sem=rel_send, recv_sem=rel_recv.at[slot], device_id=sibling, device_id_type=MESH)
        relay.start()

        def sigma_rows(base):
            def body(b, carry):
                at = pl.ds(pl.multiple_of(base + b * rb, rb), rb)
                low = pl.ds(pl.multiple_of(count + base + b * rb, rb), rb)
                gre, gim = site[0, at, :], site[1, at, :]
                qre, qim = q[slot, 0, at, :], sgn * q[slot, 1, at, :]
                rh, rl = split(gim * qim - gre * qre)
                ih, il = split(-(gre * qim + gim * qre))
                zhi[at, :] = rh
                zlo[at, :] = rl
                zhi[low, :] = ih
                zlo[low, :] = il
                return carry

            lax.fori_loop(0, hr // rb, body, 0)

        sigma_rows(mine)
        relay.wait_recv()
        sigma_rows(other)

        def inverse(step, carry):
            m, t = lax.div(step, 2), lax.rem(step, 2)
            top = pl.ds(pl.multiple_of(m * hr, hr), hr)
            bot = pl.ds(pl.multiple_of(count + m * hr, hr), hr)
            right = pl.ds(pl.multiple_of(t * (2 * width), 2 * width), 2 * width)
            z = (zhi[:, right], zlo[:, right])
            re = mm3((inv_hi[top, :], inv_lo[top, :]), z)
            im = mm3((inv_hi[bot, :], inv_lo[bot, :]), z)
            lane = lax.broadcasted_iota(jnp.int32, (hr, width), 1)
            for p in range(2):
                rep = re[:, p * width:(p + 1) * width]
                imp = im[:, p * width:(p + 1) * width]
                r0 = jnp.where(lane < half, rep, pltpu.roll(imp, half, 1))
                r1 = jnp.where(lane < half, pltpu.roll(rep, half, 1), imp)
                base = m * (hr * rows) + t * 4 + 2 * p
                put(base, hr, r0)
                put(base + 1, hr, r1)
            return carry

        lax.fori_loop(0, 4, inverse, 0)

        outs = []
        for j in range(tiles):
            outs.append(pltpu.make_async_copy(buf.at[j], recv_hbm.at[c, :, :, lanes_of(j)], stage_sem.at[j]))
            outs.append(pltpu.make_async_copy(
                buf.at[j, pl.ds(me * k_local, k_local)],
                sig_hbm.at[:, pl.ds(row_of(me, c), rows), lanes_of(j)], own_sem.at[j]))
        for out in outs:
            out.start()
        for out in outs:
            out.wait()

        def send_back(g, carry):
            for i in range(len(peers)):
                ret_copy(c, g, i).start()
            return carry

        lax.fori_loop(0, GROUP_COUNT, send_back, 0)
        gs_copy.wait_send()
        q_copy.wait_send()
        relay.wait_send()
        return carry

    lax.fori_loop(0, chunks, chunk_step, 0)

    def finish(c, carry):
        for i in range(len(peers)):
            fwd_copy(c, i).wait_send()

        def inner(g, carry):
            for i in range(len(peers)):
                ret_copy(c, g, i).wait()
            return carry

        return lax.fori_loop(0, GROUP_COUNT, inner, carry)

    lax.fori_loop(0, chunks, finish, 0)


def born_call(n, x, cosine, sine, first_len):
    k_local, full, width = x.shape
    count = n * k_local
    rows = SUBLANES
    chunks = full // n // rows
    cols = rows * width // 2
    tiles = width // LANES
    hr = count // 2
    any_spec = pl.BlockSpec(memory_space=pl.ANY)
    vmem = pl.BlockSpec(memory_space=pltpu.VMEM)
    dma = pltpu.SemaphoreType.DMA
    return pl.pallas_call(
        functools.partial(born_kernel, n, chunks, first_len),
        out_shape=(
            jax.ShapeDtypeStruct((chunks, count, rows, width), F32),
            jax.ShapeDtypeStruct(x.shape, F32),
        ),
        in_specs=[any_spec, vmem, vmem],
        out_specs=(any_spec, any_spec),
        scratch_shapes=[
            pltpu.VMEM((tiles, count, rows, LANES), F32),
            pltpu.VMEM((2, count, cols), F32),
            pltpu.VMEM((2, 2, hr, cols), F32),
            pltpu.VMEM((2, hr, cols), F32),
            pltpu.VMEM((2, 2, count, cols), F32),
            pltpu.VMEM((2 * count, cols), BF16),
            pltpu.VMEM((2 * count, cols), BF16),
            pltpu.VMEM((2 * count, 2 * count), BF16),
            pltpu.VMEM((2 * count, 2 * count), BF16),
            pltpu.VMEM((2 * count, 2 * count), BF16),
            pltpu.VMEM((2 * count, 2 * count), BF16),
            dma((chunks, n - 1)), dma((chunks, n - 1)), dma((n, tiles)),
            dma(()), dma((2,)), dma(()), dma((2,)), dma(()), dma((2,)),
            dma((chunks, GROUP_COUNT, n - 1)), dma((chunks, GROUP_COUNT, n - 1)),
            dma((tiles,)), dma((tiles,)),
        ],
        compiler_params=pltpu.CompilerParams(
            collective_id=0, has_side_effects=True, vmem_limit_bytes=67043328
        ),
        name="born",
    )(x, cosine, sine)


def on_device(green_guess, green_free, retarded, momentum_order):
    n = lax.axis_size("mom")
    k_local, full, width = green_guess.shape[1:]
    count = n * k_local
    fits = n & (n - 1) == 0 and full % (n * SUBLANES) == 0 and lax.axis_size("comp") == 4 and count % 512 == 0 and width % LANES == 0
    if not fits:
        return on_device_plain(green_guess, green_free, retarded, momentum_order)
    cosine, sine = small_tables(momentum_order, count, L1)
    _, sigma = born_call(n, green_guess[0], cosine, sine, L1)
    green, sigma = dyson_call(sigma, retarded, green_free[0])
    return green[None], sigma[None]


def solution(mesh):
    return jax.shard_map(
        on_device,
        mesh=mesh,
        in_specs=(
            P("comp", "mom", None, None),
            P("comp", "mom", None, None),
            P("mom", None, None),
            P(),
        ),
        out_specs=(P("comp", "mom", None, None), P("comp", "mom", None, None)),
        check_vma=False,
    )
```

```python
import functools
import math

import jax
import jax.numpy as jnp
from jax import lax
from jax.experimental import pallas as pl
from jax.experimental.pallas import tpu as pltpu
from jax.sharding import PartitionSpec as P

K = 512
L1 = 16


highest = lax.Precision.HIGH


def partner(x, axis, bit):
    return lax.ppermute(x, axis, [(i, i ^ 1 << bit) for i in range(lax.axis_size(axis))])


def phase_tables(momentum_order, count, first_len):
    second_len = count // first_len
    site_ids = jnp.arange(count, dtype=jnp.int32)
    site_one = site_ids // second_len
    site_two = site_ids % second_len
    mom_one = momentum_order // second_len
    mom_two = momentum_order % second_len
    phases = (
        site_one[:, None] * mom_one[None, :] * second_len
        + site_two[:, None] * mom_two[None, :] * first_len
    ) % count
    angles = phases.astype(jnp.float32) * (2.0 * math.pi / count)
    norm_factor = 1.0 / math.sqrt(count)
    return (jnp.cos(angles) * norm_factor, jnp.sin(angles) * norm_factor)


def forward_transform(values, cosine, sine_table, half_width):
    full_shape = values.shape
    flattened = values.reshape(full_shape[0], -1)
    with_cos = jnp.dot(
        cosine, flattened, precision=highest, preferred_element_type=jnp.float32
    ).reshape(full_shape)
    with_sin = jnp.dot(
        sine_table, flattened, precision=highest, preferred_element_type=jnp.float32
    ).reshape(full_shape)
    real_part = with_cos[..., :half_width] - with_sin[..., half_width:]
    imag_part = with_cos[..., half_width:] + with_sin[..., :half_width]
    return jnp.concatenate([real_part, imag_part], axis=-1)


def inverse_transform(values, cos_back, sin_back, half_width):
    full_shape = values.shape
    flattened = values.reshape(full_shape[0], -1)
    with_cos = jnp.dot(
        cos_back, flattened, precision=highest, preferred_element_type=jnp.float32
    ).reshape(full_shape)
    with_sin = jnp.dot(
        sin_back, flattened, precision=highest, preferred_element_type=jnp.float32
    ).reshape(full_shape)
    real_part = with_cos[..., :half_width] + with_sin[..., half_width:]
    imag_part = with_cos[..., half_width:] - with_sin[..., :half_width]
    return jnp.concatenate([real_part, imag_part], axis=-1)


def triple(own_part, second, conj_factor, half_width):
    prod_real = (
        own_part[..., :half_width] * second[..., :half_width]
        - own_part[..., half_width:] * second[..., half_width:]
    )
    prod_imag = (
        own_part[..., :half_width] * second[..., half_width:]
        + own_part[..., half_width:] * second[..., :half_width]
    )
    conj_real = conj_factor[..., :half_width]
    conj_imag = conj_factor[..., half_width:]
    real_part = prod_real * conj_real + prod_imag * conj_imag
    imag_part = prod_imag * conj_real - prod_real * conj_imag
    return -jnp.concatenate([real_part, imag_part], axis=-1)


def dyson(sigma_mom, retarded, free_part, half_width):
    ret_real = retarded[..., :half_width]
    ret_imag = retarded[..., half_width:]
    swapped = jnp.concatenate([-sigma_mom[..., half_width:], sigma_mom[..., :half_width]], axis=-1)
    left_prod = jnp.einsum(
        "kij,kjx->kix", ret_real, sigma_mom, precision=highest, preferred_element_type=jnp.float32
    )
    left_prod = left_prod + jnp.einsum(
        "kij,kjx->kix", ret_imag, swapped, precision=highest, preferred_element_type=jnp.float32
    )
    turned = jnp.concatenate([left_prod[..., half_width:], -left_prod[..., :half_width]], axis=-1)
    real_part = jnp.einsum(
        "kim,kjm->kij", left_prod, retarded, precision=highest, preferred_element_type=jnp.float32
    )
    imag_part = jnp.einsum(
        "kim,kjm->kij", turned, retarded, precision=highest, preferred_element_type=jnp.float32
    )
    return free_part + jnp.concatenate([real_part, imag_part], axis=-1)


CHUNKS = 3
GROUPS = 4


def exchange(send, axis):
    size = lax.axis_size(axis)
    return [send[0]] + [
        lax.ppermute(send[s], axis, [(i, i ^ s) for i in range(size)]) for s in range(1, size)
    ]


def on_device_plain(green_guess, green_free, retarded, momentum_order):
    mom_count = lax.axis_size("mom")
    me = lax.axis_index("mom")
    width = green_guess.shape[-1]
    half_width = width // 2
    k_local = green_guess.shape[1]
    tile_rows = half_width // mom_count
    rows = tile_rows // CHUNKS
    group = k_local // GROUPS
    cosine, sine_table = phase_tables(momentum_order, K, L1)
    cos_back = cosine.T
    sin_back = sine_table.T
    free_local = green_free[0]
    current = green_guess[0]

    tiled = current.reshape(k_local, mom_count, CHUNKS, rows, width)
    arrived = [
        lax.all_to_all(tiled[:, :, c], "mom", split_axis=1, concat_axis=0, tiled=True)
        for c in range(CHUNKS)
    ]
    pieces = []
    for c in range(CHUNKS):
        in_sites = forward_transform(arrived[c][:, 0], cosine, sine_table, half_width)
        spin_other = partner(in_sites, "comp", 1)
        cross_other = partner(spin_other, "comp", 0)
        sigma_sites = triple(in_sites, spin_other, cross_other, half_width)
        tile = inverse_transform(sigma_sites, cos_back, sin_back, half_width)
        pieces.append(lax.all_to_all(tile.reshape(mom_count, k_local, 1, rows, width), "mom", split_axis=0, concat_axis=2, tiled=True))
    sigma = jnp.stack(pieces, axis=3).reshape(k_local, half_width, width)
    return (dyson(sigma, retarded, free_local, half_width)[None], sigma[None])


BF16 = jnp.bfloat16
F32 = jnp.float32
SUBLANES = 8
LANES = 128
LATE_SHARE = 8
MESH = pl.DeviceIdType.MESH


def flip(index, mask, count):
    out, bit = 0, 1
    while bit < count:
        part = lax.rem(lax.div(index, bit), 2)
        out = out + bit * ((1 - part) if (mask // bit) % 2 else part)
        bit *= 2
    return out


def split(value):
    high = value.astype(BF16)
    return high, (value - high.astype(F32)).astype(BF16)


def mm(left, right, dims=((1,), (0,))):
    return lax.dot_general(left, right, (dims, ((), ())), preferred_element_type=F32)


def mm3(left, right, dims=((1,), (0,))):
    return mm(left[0], right[0], dims) + (mm(left[0], right[1], dims) + mm(left[1], right[0], dims))


def small_tables(momentum_order, count, first_len):
    second_len = count // first_len
    ids = jnp.arange(first_len + second_len, dtype=jnp.int32)[:, None]
    mom_one = (momentum_order // second_len)[None, :]
    mom_two = (momentum_order % second_len)[None, :]
    phases = jnp.where(
        ids < first_len,
        (ids * mom_one * second_len) % count,
        ((ids - first_len) * mom_two * first_len) % count,
    )
    angles = phases.astype(F32) * (2.0 * math.pi / count)
    scale = jnp.where(ids < first_len, 1.0 / math.sqrt(count), 1.0).astype(F32)
    return jnp.cos(angles) * scale, jnp.sin(angles) * scale


def stacked(left, right, dims=((1,), (0,))):
    size = left[0].shape[0]
    both = mm(jnp.concatenate(left, axis=0), right[0], dims)
    return both[:size] + (both[size:] + mm(left[0], right[1], dims))


def dyson_block(sigma, ret, free):
    half = sigma.shape[0]
    lane = lax.broadcasted_iota(jnp.int32, sigma.shape, 1)
    sign = jnp.where(lane < half, -1.0, 1.0).astype(F32)
    ret_parts = split(ret)
    sig_pair = [jnp.concatenate(p, axis=0) for p in zip(split(sigma), split(pltpu.roll(sigma, half, 1) * sign))]
    ret_pair = [jnp.concatenate(p, axis=0) for p in zip(ret_parts, split(pltpu.roll(ret, half, 1) * sign))]
    left = stacked(ret_parts, sig_pair)
    return free + stacked(split(left), ret_pair, ((1,), (1,)))


def dyson_early_kernel(sig_ref, ret_ref, free_ref, green_ref, out_ref):
    for i in range(sig_ref.shape[0]):
        sigma = sig_ref[i]
        out_ref[i] = sigma
        green_ref[i] = dyson_block(sigma, ret_ref[i], free_ref[i])


def dyson_late_kernel(sig_ref, ret_ref, free_ref, _green, _out, green_ref, out_ref):
    step = ret_ref.shape[0]
    for i in range(step):
        sigma = sig_ref[:, pl.program_id(0) * step + i].reshape(ret_ref.shape[1:])
        out_ref[i] = sigma
        green_ref[i] = dyson_block(sigma, ret_ref[i], free_ref[i])


def dyson_cost(count, half):
    return pl.CostEstimate(
        flops=count * half * half * half * 8 * 6, bytes_accessed=count * half * half * 2 * 4 * 5, transcendentals=0)


def dyson_early(sigma, retarded, free):
    early, half, width = sigma.shape
    step = math.gcd(early, 4)
    spec = pl.BlockSpec((step, half, width), lambda k: (k, 0, 0))
    shape = jax.ShapeDtypeStruct(free.shape, F32)
    return pl.pallas_call(
        dyson_early_kernel,
        grid=(early // step,),
        in_specs=[spec] * 3,
        out_specs=(spec, spec),
        out_shape=(shape, shape),
        cost_estimate=dyson_cost(early, half),
        name="dyson_early",
    )(sigma, retarded, free)


def dyson_late(pieces, retarded, free, green, sigma):
    late = pieces.shape[1]
    k_local, half, width = free.shape
    early = k_local - late
    step = math.gcd(math.gcd(early, late), 2)
    spec = pl.BlockSpec((step, half, width), lambda k: (early // step + k, 0, 0))
    any_spec = pl.BlockSpec(memory_space=pl.ANY)
    shape = jax.ShapeDtypeStruct(free.shape, F32)
    return pl.pallas_call(
        dyson_late_kernel,
        grid=(late // step,),
        in_specs=[pl.BlockSpec(memory_space=pltpu.VMEM), spec, spec, any_spec, any_spec],
        out_specs=(spec, spec),
        out_shape=(shape, shape),
        input_output_aliases={3: 0, 4: 1},
        cost_estimate=dyson_cost(late, half),
        name="dyson_late",
    )(pieces, retarded, free, green, sigma)


def born_kernel(
    n, chunks, first_len,
    x_hbm, cos_ref, sin_ref,
    recv_hbm, sig_hbm, late_hbm,
    buf, site, gs, qsend, q, zhi, zlo, fwd_hi, fwd_lo, inv_hi, inv_lo,
    fwd_send, fwd_recv, load_sem, gs_send, gs_recv, q_send, q_recv, rel_send, rel_recv, ret_send, ret_recv, own_sem, stage_sem, late_sem,
):
    me = lax.axis_index("mom")
    comp = lax.axis_index("comp")
    core = lax.rem(comp, 2)
    sibling = {"comp": comp + 1 - 2 * core}
    across = {"comp": lax.rem(comp + 2, 4)}
    sgn = (1 - 2 * core).astype(F32)
    k_local, full, width = x_hbm.shape
    half = width // 2
    count = n * k_local
    rows = SUBLANES
    pairs = rows // 2
    cols = pairs * width
    second_len = count // first_len
    early = sig_hbm.shape[0]
    late = k_local - early
    masks = list(range(n // 2, n)) + list(range(1, n // 2))
    peers = [flip(me, s, n) for s in masks]
    hr = count // 2

    barrier = pltpu.get_barrier_semaphore()
    for peer in peers:
        pl.semaphore_signal(barrier, inc=1, device_id={"mom": peer}, device_id_type=MESH)
    pl.semaphore_signal(barrier, inc=1, device_id=sibling, device_id_type=MESH)
    pl.semaphore_signal(barrier, inc=1, device_id=across, device_id_type=MESH)
    pl.semaphore_wait(barrier, len(peers) + 2)

    def row_of(device, c):
        return pl.multiple_of((device * chunks + c) * rows, rows)

    def fwd_copy(c, i):
        return pltpu.make_async_remote_copy(
            src_ref=x_hbm.at[:, pl.ds(row_of(peers[i], c), rows), :],
            dst_ref=recv_hbm.at[c, pl.ds(me * k_local, k_local)],
            send_sem=fwd_send.at[c, i], recv_sem=fwd_recv.at[c, i],
            device_id={"mom": peers[i]}, device_id_type=MESH)

    def ret_copy(c, i):
        return pltpu.make_async_remote_copy(
            src_ref=recv_hbm.at[c, pl.ds(peers[i] * k_local, early)],
            dst_ref=sig_hbm.at[:, pl.ds(row_of(me, c), rows), :],
            send_sem=ret_send.at[c, i], recv_sem=ret_recv.at[c, i],
            device_id={"mom": peers[i]}, device_id_type=MESH)

    def send_forward(c, carry):
        for i in range(len(peers)):
            fwd_copy(c, i).start()
        return carry

    lax.fori_loop(0, chunks, send_forward, 0)

    def build(one, carry):
        c1 = cos_ref[pl.ds(one, 1), :]
        s1 = sin_ref[pl.ds(one, 1), :]
        c2 = cos_ref[pl.ds(first_len, second_len), :]
        s2 = sin_ref[pl.ds(first_len, second_len), :]
        at = pl.ds(pl.multiple_of(one * second_len, second_len), second_len)
        low = pl.ds(pl.multiple_of(count + one * second_len, second_len), second_len)
        cosine = c1 * c2 - s1 * s2
        sine = s1 * c2 + c1 * s2
        site[0, at, 0:count] = cosine
        site[1, at, 0:count] = sine
        ch, cl = split(cosine)
        sh, sl = split(sine)
        for ref, cv, sv in ((fwd_hi, ch, sh), (fwd_lo, cl, sl)):
            ref[at, 0:count] = cv
            ref[at, count:2 * count] = -sv
            ref[low, 0:count] = sv
            ref[low, count:2 * count] = cv
        return carry

    lax.fori_loop(0, first_len, build, 0)

    def turn(b, carry):
        at = pl.ds(pl.multiple_of(b * 128, 128), 128)
        low = pl.ds(pl.multiple_of(count + b * 128, 128), 128)
        ch, cl = split(site[0, :, at].T)
        sh, sl = split(site[1, :, at].T)
        for ref, cv, sv in ((inv_hi, ch, sh), (inv_lo, cl, sl)):
            ref[at, 0:count] = cv
            ref[at, count:2 * count] = sv
            ref[low, 0:count] = -sv
            ref[low, count:2 * count] = cv
        return carry

    lax.fori_loop(0, count // 128, turn, 0)

    tiles = width // LANES
    flat = buf.reshape(tiles, count * rows, LANES)
    by_owner = buf.reshape(tiles, n, k_local, rows, LANES)

    def take(start, size):
        return jnp.concatenate([flat[j, pl.ds(start, size, stride=rows), :] for j in range(tiles)], axis=1)

    def put(start, size, value):
        for j in range(tiles):
            flat[j, pl.ds(start, size, stride=rows), :] = value[:, j * LANES:(j + 1) * LANES]

    def lanes_of(j):
        return pl.ds(j * LANES, LANES)


    def chunk_step(c, carry):
        slot = lax.rem(c, 2)
        loads = []
        for j in range(tiles):
            loads.append(pltpu.make_async_copy(
                x_hbm.at[:, pl.ds(row_of(me, c), rows), lanes_of(j)],
                buf.at[j, pl.ds(me * k_local, k_local)], load_sem.at[n - 1, j]))
            loads[-1].start()
        for i in range(len(peers)):
            fwd_copy(c, i).wait_recv()
            at = pl.ds(peers[i] * k_local, k_local)
            for j in range(tiles):
                loads.append(pltpu.make_async_copy(
                    recv_hbm.at[c, at, :, lanes_of(j)], buf.at[j, at], load_sem.at[i, j]))
                loads[-1].start()
        for load in loads:
            load.wait()

        kb = k_local

        def stage(b, carry):
            lane = lax.broadcasted_iota(jnp.int32, (kb, width), 1)
            at = pl.ds(pl.multiple_of(b * kb, kb), kb)
            low = pl.ds(pl.multiple_of(count + b * kb, kb), kb)
            for p in range(pairs):
                r0 = take(b * (kb * rows) + 2 * p, kb)
                r1 = take(b * (kb * rows) + 2 * p + 1, kb)
                re = jnp.where(lane < half, r0, pltpu.roll(r1, half, 1))
                im = jnp.where(lane < half, pltpu.roll(r0, half, 1), r1)
                here = pl.ds(p * width, width)
                rh, rl = split(re)
                ih, il = split(im)
                zhi[at, here] = rh
                zlo[at, here] = rl
                zhi[low, here] = ih
                zlo[low, here] = il
            return carry

        lax.fori_loop(0, count // kb, stage, 0)

        def forward(step, carry):
            m, t = lax.div(step, 3), lax.rem(step, 3)
            plane, part = lax.div(m, 2), lax.rem(m, 2)
            left = pl.ds(pl.multiple_of(m * hr, hr), hr)
            right = pl.ds(pl.multiple_of(t * (cols // 3), cols // 3), cols // 3)
            value = mm3((fwd_hi[left, :], fwd_lo[left, :]), (zhi[:, right], zlo[:, right]))
            site[plane, pl.ds(pl.multiple_of(part * hr, hr), hr), right] = value
            return carry

        lax.fori_loop(0, 12, forward, 0)

        mine = pl.multiple_of(core * hr, hr)
        other = pl.multiple_of((1 - core) * hr, hr)
        gs_copy = pltpu.make_async_remote_copy(
            src_ref=site.at[:, pl.ds(other, hr), :], dst_ref=gs.at[slot],
            send_sem=gs_send, recv_sem=gs_recv.at[slot], device_id=sibling, device_id_type=MESH)
        gs_copy.start()
        gs_copy.wait_recv()

        rb = 16

        def pair(b, carry):
            here = pl.ds(pl.multiple_of(b * rb, rb), rb)
            at = pl.ds(pl.multiple_of(mine + b * rb, rb), rb)
            ore, oim = site[0, at, :], site[1, at, :]
            sre, sim = gs[slot, 0, here, :], gs[slot, 1, here, :]
            qsend[0, here, :] = ore * sre + oim * sim
            qsend[1, here, :] = sgn * (oim * sre - ore * sim)
            return carry

        lax.fori_loop(0, hr // rb, pair, 0)

        q_copy = pltpu.make_async_remote_copy(
            src_ref=qsend, dst_ref=q.at[slot, :, pl.ds(mine, hr), :],
            send_sem=q_send, recv_sem=q_recv.at[slot], device_id=across, device_id_type=MESH)
        q_copy.start()
        q_copy.wait_recv()
        relay = pltpu.make_async_remote_copy(
            src_ref=q.at[slot, :, pl.ds(mine, hr), :], dst_ref=q.at[slot, :, pl.ds(mine, hr), :],
            send_sem=rel_send, recv_sem=rel_recv.at[slot], device_id=sibling, device_id_type=MESH)
        relay.start()

        def sigma_rows(base):
            def body(b, carry):
                at = pl.ds(pl.multiple_of(base + b * rb, rb), rb)
                low = pl.ds(pl.multiple_of(count + base + b * rb, rb), rb)
                gre, gim = site[0, at, :], site[1, at, :]
                qre, qim = q[slot, 0, at, :], sgn * q[slot, 1, at, :]
                rh, rl = split(gim * qim - gre * qre)
                ih, il = split(-(gre * qim + gim * qre))
                zhi[at, :] = rh
                zlo[at, :] = rl
                zhi[low, :] = ih
                zlo[low, :] = il
                return carry

            lax.fori_loop(0, hr // rb, body, 0)

        sigma_rows(mine)
        relay.wait_recv()
        sigma_rows(other)

        def inverse(step, carry):
            m, t = lax.div(step, 2), lax.rem(step, 2)
            top = pl.ds(pl.multiple_of(m * hr, hr), hr)
            bot = pl.ds(pl.multiple_of(count + m * hr, hr), hr)
            right = pl.ds(pl.multiple_of(t * (2 * width), 2 * width), 2 * width)
            z = (zhi[:, right], zlo[:, right])
            re = mm3((inv_hi[top, :], inv_lo[top, :]), z)
            im = mm3((inv_hi[bot, :], inv_lo[bot, :]), z)
            lane = lax.broadcasted_iota(jnp.int32, (hr, width), 1)
            for p in range(2):
                rep = re[:, p * width:(p + 1) * width]
                imp = im[:, p * width:(p + 1) * width]
                r0 = jnp.where(lane < half, rep, pltpu.roll(imp, half, 1))
                r1 = jnp.where(lane < half, pltpu.roll(rep, half, 1), imp)
                base = m * (hr * rows) + t * 4 + 2 * p
                put(base, hr, r0)
                put(base + 1, hr, r1)
            return carry

        lax.fori_loop(0, 4, inverse, 0)

        outs = []
        for j in range(tiles):
            outs.append(pltpu.make_async_copy(buf.at[j], recv_hbm.at[c, :, :, lanes_of(j)], stage_sem.at[j]))
            outs.append(pltpu.make_async_copy(
                buf.at[j, pl.ds(me * k_local, early)],
                sig_hbm.at[:, pl.ds(row_of(me, c), rows), lanes_of(j)], own_sem.at[j]))
            outs.append(pltpu.make_async_copy(
                by_owner.at[j, :, pl.ds(early, late)],
                late_hbm.at[:, :, pl.ds(pl.multiple_of(c * rows, rows), rows), lanes_of(j)], late_sem.at[j]))
        for out in outs:
            out.start()
        for out in outs:
            out.wait()

        for i in range(len(peers)):
            ret_copy(c, i).start()
        gs_copy.wait_send()
        q_copy.wait_send()
        relay.wait_send()
        return carry

    lax.fori_loop(0, chunks, chunk_step, 0)

    def finish(c, carry):
        for i in range(len(peers)):
            fwd_copy(c, i).wait_send()
            ret_copy(c, i).wait()
        return carry

    lax.fori_loop(0, chunks, finish, 0)


def born_call(n, x, cosine, sine, first_len):
    k_local, full, width = x.shape
    count = n * k_local
    rows = SUBLANES
    chunks = full // n // rows
    cols = rows * width // 2
    tiles = width // LANES
    hr = count // 2
    late = k_local // LATE_SHARE
    any_spec = pl.BlockSpec(memory_space=pl.ANY)
    vmem = pl.BlockSpec(memory_space=pltpu.VMEM)
    dma = pltpu.SemaphoreType.DMA
    return pl.pallas_call(
        functools.partial(born_kernel, n, chunks, first_len),
        out_shape=(
            jax.ShapeDtypeStruct((chunks, count, rows, width), F32),
            jax.ShapeDtypeStruct((k_local - late, full, width), F32),
            jax.ShapeDtypeStruct((n, late, full // n, width), F32),
        ),
        in_specs=[any_spec, vmem, vmem],
        out_specs=(any_spec, any_spec, any_spec),
        scratch_shapes=[
            pltpu.VMEM((tiles, count, rows, LANES), F32),
            pltpu.VMEM((2, count, cols), F32),
            pltpu.VMEM((2, 2, hr, cols), F32),
            pltpu.VMEM((2, hr, cols), F32),
            pltpu.VMEM((2, 2, count, cols), F32),
            pltpu.VMEM((2 * count, cols), BF16),
            pltpu.VMEM((2 * count, cols), BF16),
            pltpu.VMEM((2 * count, 2 * count), BF16),
            pltpu.VMEM((2 * count, 2 * count), BF16),
            pltpu.VMEM((2 * count, 2 * count), BF16),
            pltpu.VMEM((2 * count, 2 * count), BF16),
            dma((chunks, n - 1)), dma((chunks, n - 1)), dma((n, tiles)),
            dma(()), dma((2,)), dma(()), dma((2,)), dma(()), dma((2,)),
            dma((chunks, n - 1)), dma((chunks, n - 1)),
            dma((tiles,)), dma((tiles,)), dma((tiles,)),
        ],
        compiler_params=pltpu.CompilerParams(
            collective_id=0, has_side_effects=True, vmem_limit_bytes=67043328
        ),
        name="born",
    )(x, cosine, sine)


def on_device(green_guess, green_free, retarded, momentum_order):
    n = lax.axis_size("mom")
    k_local, full, width = green_guess.shape[1:]
    count = n * k_local
    fits = n & (n - 1) == 0 and full % (n * SUBLANES) == 0 and lax.axis_size("comp") == 4 and count % 512 == 0 and width % LANES == 0 and k_local % LATE_SHARE == 0
    if not fits:
        return on_device_plain(green_guess, green_free, retarded, momentum_order)
    cosine, sine = small_tables(momentum_order, count, L1)
    _, sigma, late = born_call(n, green_guess[0], cosine, sine, L1)
    pieces = lax.all_to_all(late, "mom", split_axis=0, concat_axis=0, tiled=True)
    green, sigma = dyson_early(sigma, retarded, green_free[0])
    green, sigma = dyson_late(pieces, retarded, green_free[0], green, sigma)
    return green[None], sigma[None]


def solution(mesh):
    return jax.shard_map(
        on_device,
        mesh=mesh,
        in_specs=(
            P("comp", "mom", None, None),
            P("comp", "mom", None, None),
            P("mom", None, None),
            P(),
        ),
        out_specs=(P("comp", "mom", None, None), P("comp", "mom", None, None)),
        check_vma=False,
    )
```

```python
import functools
import math

import jax
import jax.numpy as jnp
from jax import lax
from jax.experimental import pallas as pl
from jax.experimental.pallas import tpu as pltpu
from jax.sharding import PartitionSpec as P

K = 512
L1 = 16


highest = lax.Precision.HIGH


def partner(x, axis, bit):
    return lax.ppermute(x, axis, [(i, i ^ 1 << bit) for i in range(lax.axis_size(axis))])


def phase_tables(momentum_order, count, first_len):
    second_len = count // first_len
    site_ids = jnp.arange(count, dtype=jnp.int32)
    site_one = site_ids // second_len
    site_two = site_ids % second_len
    mom_one = momentum_order // second_len
    mom_two = momentum_order % second_len
    phases = (
        site_one[:, None] * mom_one[None, :] * second_len
        + site_two[:, None] * mom_two[None, :] * first_len
    ) % count
    angles = phases.astype(jnp.float32) * (2.0 * math.pi / count)
    norm_factor = 1.0 / math.sqrt(count)
    return (jnp.cos(angles) * norm_factor, jnp.sin(angles) * norm_factor)


def forward_transform(values, cosine, sine_table, half_width):
    full_shape = values.shape
    flattened = values.reshape(full_shape[0], -1)
    with_cos = jnp.dot(
        cosine, flattened, precision=highest, preferred_element_type=jnp.float32
    ).reshape(full_shape)
    with_sin = jnp.dot(
        sine_table, flattened, precision=highest, preferred_element_type=jnp.float32
    ).reshape(full_shape)
    real_part = with_cos[..., :half_width] - with_sin[..., half_width:]
    imag_part = with_cos[..., half_width:] + with_sin[..., :half_width]
    return jnp.concatenate([real_part, imag_part], axis=-1)


def inverse_transform(values, cos_back, sin_back, half_width):
    full_shape = values.shape
    flattened = values.reshape(full_shape[0], -1)
    with_cos = jnp.dot(
        cos_back, flattened, precision=highest, preferred_element_type=jnp.float32
    ).reshape(full_shape)
    with_sin = jnp.dot(
        sin_back, flattened, precision=highest, preferred_element_type=jnp.float32
    ).reshape(full_shape)
    real_part = with_cos[..., :half_width] + with_sin[..., half_width:]
    imag_part = with_cos[..., half_width:] - with_sin[..., :half_width]
    return jnp.concatenate([real_part, imag_part], axis=-1)


def triple(own_part, second, conj_factor, half_width):
    prod_real = (
        own_part[..., :half_width] * second[..., :half_width]
        - own_part[..., half_width:] * second[..., half_width:]
    )
    prod_imag = (
        own_part[..., :half_width] * second[..., half_width:]
        + own_part[..., half_width:] * second[..., :half_width]
    )
    conj_real = conj_factor[..., :half_width]
    conj_imag = conj_factor[..., half_width:]
    real_part = prod_real * conj_real + prod_imag * conj_imag
    imag_part = prod_imag * conj_real - prod_real * conj_imag
    return -jnp.concatenate([real_part, imag_part], axis=-1)


def dyson(sigma_mom, retarded, free_part, half_width):
    ret_real = retarded[..., :half_width]
    ret_imag = retarded[..., half_width:]
    swapped = jnp.concatenate([-sigma_mom[..., half_width:], sigma_mom[..., :half_width]], axis=-1)
    left_prod = jnp.einsum(
        "kij,kjx->kix", ret_real, sigma_mom, precision=highest, preferred_element_type=jnp.float32
    )
    left_prod = left_prod + jnp.einsum(
        "kij,kjx->kix", ret_imag, swapped, precision=highest, preferred_element_type=jnp.float32
    )
    turned = jnp.concatenate([left_prod[..., half_width:], -left_prod[..., :half_width]], axis=-1)
    real_part = jnp.einsum(
        "kim,kjm->kij", left_prod, retarded, precision=highest, preferred_element_type=jnp.float32
    )
    imag_part = jnp.einsum(
        "kim,kjm->kij", turned, retarded, precision=highest, preferred_element_type=jnp.float32
    )
    return free_part + jnp.concatenate([real_part, imag_part], axis=-1)


CHUNKS = 3
GROUPS = 4


def exchange(send, axis):
    size = lax.axis_size(axis)
    return [send[0]] + [
        lax.ppermute(send[s], axis, [(i, i ^ s) for i in range(size)]) for s in range(1, size)
    ]


def on_device_plain(green_guess, green_free, retarded, momentum_order):
    mom_count = lax.axis_size("mom")
    me = lax.axis_index("mom")
    width = green_guess.shape[-1]
    half_width = width // 2
    k_local = green_guess.shape[1]
    tile_rows = half_width // mom_count
    rows = tile_rows // CHUNKS
    group = k_local // GROUPS
    cosine, sine_table = phase_tables(momentum_order, K, L1)
    cos_back = cosine.T
    sin_back = sine_table.T
    free_local = green_free[0]
    current = green_guess[0]

    tiled = current.reshape(k_local, mom_count, CHUNKS, rows, width)
    arrived = [
        lax.all_to_all(tiled[:, :, c], "mom", split_axis=1, concat_axis=0, tiled=True)
        for c in range(CHUNKS)
    ]
    pieces = []
    for c in range(CHUNKS):
        in_sites = forward_transform(arrived[c][:, 0], cosine, sine_table, half_width)
        spin_other = partner(in_sites, "comp", 1)
        cross_other = partner(spin_other, "comp", 0)
        sigma_sites = triple(in_sites, spin_other, cross_other, half_width)
        tile = inverse_transform(sigma_sites, cos_back, sin_back, half_width)
        pieces.append(lax.all_to_all(tile.reshape(mom_count, k_local, 1, rows, width), "mom", split_axis=0, concat_axis=2, tiled=True))
    sigma = jnp.stack(pieces, axis=3).reshape(k_local, half_width, width)
    return (dyson(sigma, retarded, free_local, half_width)[None], sigma[None])


BF16 = jnp.bfloat16
F32 = jnp.float32
SUBLANES = 8
LANES = 128
LATE_SHARE = 8
MESH = pl.DeviceIdType.MESH


def flip(index, mask, count):
    out, bit = 0, 1
    while bit < count:
        part, turn = lax.rem(lax.div(index, bit), 2), lax.rem(lax.div(mask, bit), 2)
        out = out + bit * (part + turn - 2 * part * turn)
        bit *= 2
    return out


def send_orders(count):
    up, half = [], count // 2
    while half:
        up += range(half, 2 * half)
        half //= 2
    return up, list(range(count - 1, 0, -1))


def split(value):
    high = value.astype(BF16)
    return high, (value - high.astype(F32)).astype(BF16)


def mm(left, right, dims=((1,), (0,))):
    return lax.dot_general(left, right, (dims, ((), ())), preferred_element_type=F32)


def mm3(left, right, dims=((1,), (0,))):
    return mm(left[0], right[0], dims) + (mm(left[0], right[1], dims) + mm(left[1], right[0], dims))


def small_tables(momentum_order, count, first_len):
    second_len = count // first_len
    ids = jnp.arange(first_len + second_len, dtype=jnp.int32)[:, None]
    mom_one = (momentum_order // second_len)[None, :]
    mom_two = (momentum_order % second_len)[None, :]
    phases = jnp.where(
        ids < first_len,
        (ids * mom_one * second_len) % count,
        ((ids - first_len) * mom_two * first_len) % count,
    )
    angles = phases.astype(F32) * (2.0 * math.pi / count)
    scale = jnp.where(ids < first_len, 1.0 / math.sqrt(count), 1.0).astype(F32)
    return jnp.cos(angles) * scale, jnp.sin(angles) * scale


def stacked(left, right, dims=((1,), (0,))):
    size = left[0].shape[0]
    both = mm(jnp.concatenate(left, axis=0), right[0], dims)
    return both[:size] + (both[size:] + mm(left[0], right[1], dims))


def dyson_block(sigma, ret, free):
    half = sigma.shape[0]
    lane = lax.broadcasted_iota(jnp.int32, sigma.shape, 1)
    sign = jnp.where(lane < half, -1.0, 1.0).astype(F32)
    ret_parts = split(ret)
    sig_pair = [jnp.concatenate(p, axis=0) for p in zip(split(sigma), split(pltpu.roll(sigma, half, 1) * sign))]
    ret_pair = [jnp.concatenate(p, axis=0) for p in zip(ret_parts, split(pltpu.roll(ret, half, 1) * sign))]
    left = stacked(ret_parts, sig_pair)
    return free + stacked(split(left), ret_pair, ((1,), (1,)))


def dyson_early_kernel(sig_ref, ret_ref, free_ref, green_ref, out_ref):
    for i in range(sig_ref.shape[0]):
        sigma = sig_ref[i]
        out_ref[i] = sigma
        green_ref[i] = dyson_block(sigma, ret_ref[i], free_ref[i])


def dyson_late_kernel(sig_ref, ret_ref, free_ref, _green, _out, green_ref, out_ref):
    step = ret_ref.shape[0]
    for i in range(step):
        sigma = sig_ref[:, pl.program_id(0) * step + i].reshape(ret_ref.shape[1:])
        out_ref[i] = sigma
        green_ref[i] = dyson_block(sigma, ret_ref[i], free_ref[i])


def dyson_cost(count, half):
    return pl.CostEstimate(
        flops=count * half * half * half * 8 * 6, bytes_accessed=count * half * half * 2 * 4 * 5, transcendentals=0)


def dyson_early(sigma, retarded, free):
    early, half, width = sigma.shape
    step = math.gcd(early, 4)
    spec = pl.BlockSpec((step, half, width), lambda k: (k, 0, 0))
    shape = jax.ShapeDtypeStruct(free.shape, F32)
    return pl.pallas_call(
        dyson_early_kernel,
        grid=(early // step,),
        in_specs=[spec] * 3,
        out_specs=(spec, spec),
        out_shape=(shape, shape),
        cost_estimate=dyson_cost(early, half),
        name="dyson_early",
    )(sigma, retarded, free)


def dyson_late(pieces, retarded, free, green, sigma):
    late = pieces.shape[1]
    k_local, half, width = free.shape
    early = k_local - late
    step = math.gcd(math.gcd(early, late), 2)
    spec = pl.BlockSpec((step, half, width), lambda k: (early // step + k, 0, 0))
    any_spec = pl.BlockSpec(memory_space=pl.ANY)
    shape = jax.ShapeDtypeStruct(free.shape, F32)
    return pl.pallas_call(
        dyson_late_kernel,
        grid=(late // step,),
        in_specs=[pl.BlockSpec(memory_space=pltpu.VMEM), spec, spec, any_spec, any_spec],
        out_specs=(spec, spec),
        out_shape=(shape, shape),
        input_output_aliases={3: 0, 4: 1},
        cost_estimate=dyson_cost(late, half),
        name="dyson_late",
    )(pieces, retarded, free, green, sigma)


def born_kernel(
    n, chunks, first_len,
    x_hbm, cos_ref, sin_ref,
    recv_hbm, sig_hbm, late_hbm,
    buf, site, gs, qsend, q, zhi, zlo, fwd_hi, fwd_lo, inv_hi, inv_lo,
    fwd_send, fwd_recv, load_sem, gs_send, gs_recv, q_send, q_recv, rel_send, rel_recv, ret_send, ret_recv, own_sem, stage_sem, late_sem,
):
    me = lax.axis_index("mom")
    comp = lax.axis_index("comp")
    core = lax.rem(comp, 2)
    sibling = {"comp": comp + 1 - 2 * core}
    across = {"comp": lax.rem(comp + 2, 4)}
    sgn = (1 - 2 * core).astype(F32)
    k_local, full, width = x_hbm.shape
    half = width // 2
    count = n * k_local
    rows = SUBLANES
    pairs = rows // 2
    cols = pairs * width
    second_len = count // first_len
    early = sig_hbm.shape[0]
    late = k_local - early
    peers = [flip(me, a + core * (b - a), n) for a, b in zip(*send_orders(n))]
    hr = count // 2

    barrier = pltpu.get_barrier_semaphore()
    for peer in peers:
        pl.semaphore_signal(barrier, inc=1, device_id={"mom": peer}, device_id_type=MESH)
    pl.semaphore_signal(barrier, inc=1, device_id=sibling, device_id_type=MESH)
    pl.semaphore_signal(barrier, inc=1, device_id=across, device_id_type=MESH)
    pl.semaphore_wait(barrier, len(peers) + 2)

    def row_of(device, c):
        return pl.multiple_of((device * chunks + c) * rows, rows)

    def fwd_copy(c, i):
        return pltpu.make_async_remote_copy(
            src_ref=x_hbm.at[:, pl.ds(row_of(peers[i], c), rows), :],
            dst_ref=recv_hbm.at[c, pl.ds(me * k_local, k_local)],
            send_sem=fwd_send.at[c, i], recv_sem=fwd_recv.at[c, i],
            device_id={"mom": peers[i]}, device_id_type=MESH)

    def ret_copy(c, i):
        return pltpu.make_async_remote_copy(
            src_ref=recv_hbm.at[c, pl.ds(peers[i] * k_local, early)],
            dst_ref=sig_hbm.at[:, pl.ds(row_of(me, c), rows), :],
            send_sem=ret_send.at[c, i], recv_sem=ret_recv.at[c, i],
            device_id={"mom": peers[i]}, device_id_type=MESH)

    def send_forward(c, carry):
        for i in range(len(peers)):
            fwd_copy(c, i).start()
        return carry

    lax.fori_loop(0, chunks, send_forward, 0)

    def build(one, carry):
        c1 = cos_ref[pl.ds(one, 1), :]
        s1 = sin_ref[pl.ds(one, 1), :]
        c2 = cos_ref[pl.ds(first_len, second_len), :]
        s2 = sin_ref[pl.ds(first_len, second_len), :]
        at = pl.ds(pl.multiple_of(one * second_len, second_len), second_len)
        low = pl.ds(pl.multiple_of(count + one * second_len, second_len), second_len)
        cosine = c1 * c2 - s1 * s2
        sine = s1 * c2 + c1 * s2
        site[0, at, 0:count] = cosine
        site[1, at, 0:count] = sine
        ch, cl = split(cosine)
        sh, sl = split(sine)
        for ref, cv, sv in ((fwd_hi, ch, sh), (fwd_lo, cl, sl)):
            ref[at, 0:count] = cv
            ref[at, count:2 * count] = -sv
            ref[low, 0:count] = sv
            ref[low, count:2 * count] = cv
        return carry

    lax.fori_loop(0, first_len, build, 0)

    def turn(b, carry):
        at = pl.ds(pl.multiple_of(b * 128, 128), 128)
        low = pl.ds(pl.multiple_of(count + b * 128, 128), 128)
        ch, cl = split(site[0, :, at].T)
        sh, sl = split(site[1, :, at].T)
        for ref, cv, sv in ((inv_hi, ch, sh), (inv_lo, cl, sl)):
            ref[at, 0:count] = cv
            ref[at, count:2 * count] = sv
            ref[low, 0:count] = -sv
            ref[low, count:2 * count] = cv
        return carry

    lax.fori_loop(0, count // 128, turn, 0)

    tiles = width // LANES
    flat = buf.reshape(tiles, count * rows, LANES)
    by_owner = buf.reshape(tiles, n, k_local, rows, LANES)

    def take(start, size):
        return jnp.concatenate([flat[j, pl.ds(start, size, stride=rows), :] for j in range(tiles)], axis=1)

    def put(start, size, value):
        for j in range(tiles):
            flat[j, pl.ds(start, size, stride=rows), :] = value[:, j * LANES:(j + 1) * LANES]

    def lanes_of(j):
        return pl.ds(j * LANES, LANES)


    def chunk_step(c, carry):
        slot = lax.rem(c, 2)
        loads = []
        for j in range(tiles):
            loads.append(pltpu.make_async_copy(
                x_hbm.at[:, pl.ds(row_of(me, c), rows), lanes_of(j)],
                buf.at[j, pl.ds(me * k_local, k_local)], load_sem.at[n - 1, j]))
            loads[-1].start()
        for i in range(len(peers)):
            fwd_copy(c, i).wait_recv()
            at = pl.ds(peers[i] * k_local, k_local)
            for j in range(tiles):
                loads.append(pltpu.make_async_copy(
                    recv_hbm.at[c, at, :, lanes_of(j)], buf.at[j, at], load_sem.at[i, j]))
                loads[-1].start()
        for load in loads:
            load.wait()

        kb = k_local

        def stage(b, carry):
            lane = lax.broadcasted_iota(jnp.int32, (kb, width), 1)
            at = pl.ds(pl.multiple_of(b * kb, kb), kb)
            low = pl.ds(pl.multiple_of(count + b * kb, kb), kb)
            for p in range(pairs):
                r0 = take(b * (kb * rows) + 2 * p, kb)
                r1 = take(b * (kb * rows) + 2 * p + 1, kb)
                re = jnp.where(lane < half, r0, pltpu.roll(r1, half, 1))
                im = jnp.where(lane < half, pltpu.roll(r0, half, 1), r1)
                here = pl.ds(p * width, width)
                rh, rl = split(re)
                ih, il = split(im)
                zhi[at, here] = rh
                zlo[at, here] = rl
                zhi[low, here] = ih
                zlo[low, here] = il
            return carry

        lax.fori_loop(0, count // kb, stage, 0)

        def forward(step, carry):
            m, t = lax.div(step, 3), lax.rem(step, 3)
            plane, part = lax.div(m, 2), lax.rem(m, 2)
            left = pl.ds(pl.multiple_of(m * hr, hr), hr)
            right = pl.ds(pl.multiple_of(t * (cols // 3), cols // 3), cols // 3)
            value = mm3((fwd_hi[left, :], fwd_lo[left, :]), (zhi[:, right], zlo[:, right]))
            site[plane, pl.ds(pl.multiple_of(part * hr, hr), hr), right] = value
            return carry

        lax.fori_loop(0, 12, forward, 0)

        mine = pl.multiple_of(core * hr, hr)
        other = pl.multiple_of((1 - core) * hr, hr)
        gs_copy = pltpu.make_async_remote_copy(
            src_ref=site.at[:, pl.ds(other, hr), :], dst_ref=gs.at[slot],
            send_sem=gs_send, recv_sem=gs_recv.at[slot], device_id=sibling, device_id_type=MESH)
        gs_copy.start()
        gs_copy.wait_recv()

        rb = 16

        def pair(b, carry):
            here = pl.ds(pl.multiple_of(b * rb, rb), rb)
            at = pl.ds(pl.multiple_of(mine + b * rb, rb), rb)
            ore, oim = site[0, at, :], site[1, at, :]
            sre, sim = gs[slot, 0, here, :], gs[slot, 1, here, :]
            qsend[0, here, :] = ore * sre + oim * sim
            qsend[1, here, :] = sgn * (oim * sre - ore * sim)
            return carry

        lax.fori_loop(0, hr // rb, pair, 0)

        q_copy = pltpu.make_async_remote_copy(
            src_ref=qsend, dst_ref=q.at[slot, :, pl.ds(mine, hr), :],
            send_sem=q_send, recv_sem=q_recv.at[slot], device_id=across, device_id_type=MESH)
        q_copy.start()
        q_copy.wait_recv()
        relay = pltpu.make_async_remote_copy(
            src_ref=q.at[slot, :, pl.ds(mine, hr), :], dst_ref=q.at[slot, :, pl.ds(mine, hr), :],
            send_sem=rel_send, recv_sem=rel_recv.at[slot], device_id=sibling, device_id_type=MESH)
        relay.start()

        def sigma_rows(base):
            def body(b, carry):
                at = pl.ds(pl.multiple_of(base + b * rb, rb), rb)
                low = pl.ds(pl.multiple_of(count + base + b * rb, rb), rb)
                gre, gim = site[0, at, :], site[1, at, :]
                qre, qim = q[slot, 0, at, :], sgn * q[slot, 1, at, :]
                rh, rl = split(gim * qim - gre * qre)
                ih, il = split(-(gre * qim + gim * qre))
                zhi[at, :] = rh
                zlo[at, :] = rl
                zhi[low, :] = ih
                zlo[low, :] = il
                return carry

            lax.fori_loop(0, hr // rb, body, 0)

        sigma_rows(mine)
        relay.wait_recv()
        sigma_rows(other)

        def inverse(step, carry):
            m, t = lax.div(step, 2), lax.rem(step, 2)
            top = pl.ds(pl.multiple_of(m * hr, hr), hr)
            bot = pl.ds(pl.multiple_of(count + m * hr, hr), hr)
            right = pl.ds(pl.multiple_of(t * (2 * width), 2 * width), 2 * width)
            z = (zhi[:, right], zlo[:, right])
            re = mm3((inv_hi[top, :], inv_lo[top, :]), z)
            im = mm3((inv_hi[bot, :], inv_lo[bot, :]), z)
            lane = lax.broadcasted_iota(jnp.int32, (hr, width), 1)
            for p in range(2):
                rep = re[:, p * width:(p + 1) * width]
                imp = im[:, p * width:(p + 1) * width]
                r0 = jnp.where(lane < half, rep, pltpu.roll(imp, half, 1))
                r1 = jnp.where(lane < half, pltpu.roll(rep, half, 1), imp)
                base = m * (hr * rows) + t * 4 + 2 * p
                put(base, hr, r0)
                put(base + 1, hr, r1)
            return carry

        lax.fori_loop(0, 4, inverse, 0)

        outs = []
        for j in range(tiles):
            outs.append(pltpu.make_async_copy(buf.at[j], recv_hbm.at[c, :, :, lanes_of(j)], stage_sem.at[j]))
            outs.append(pltpu.make_async_copy(
                buf.at[j, pl.ds(me * k_local, early)],
                sig_hbm.at[:, pl.ds(row_of(me, c), rows), lanes_of(j)], own_sem.at[j]))
            outs.append(pltpu.make_async_copy(
                by_owner.at[j, :, pl.ds(early, late)],
                late_hbm.at[:, :, pl.ds(pl.multiple_of(c * rows, rows), rows), lanes_of(j)], late_sem.at[j]))
        for out in outs:
            out.start()
        for out in outs:
            out.wait()

        for i in range(len(peers)):
            ret_copy(c, i).start()
        gs_copy.wait_send()
        q_copy.wait_send()
        relay.wait_send()
        return carry

    lax.fori_loop(0, chunks, chunk_step, 0)

    def finish(c, carry):
        for i in range(len(peers)):
            fwd_copy(c, i).wait_send()
            ret_copy(c, i).wait()
        return carry

    lax.fori_loop(0, chunks, finish, 0)


def born_call(n, x, cosine, sine, first_len):
    k_local, full, width = x.shape
    count = n * k_local
    rows = SUBLANES
    chunks = full // n // rows
    cols = rows * width // 2
    tiles = width // LANES
    hr = count // 2
    late = k_local // LATE_SHARE
    any_spec = pl.BlockSpec(memory_space=pl.ANY)
    vmem = pl.BlockSpec(memory_space=pltpu.VMEM)
    dma = pltpu.SemaphoreType.DMA
    return pl.pallas_call(
        functools.partial(born_kernel, n, chunks, first_len),
        out_shape=(
            jax.ShapeDtypeStruct((chunks, count, rows, width), F32),
            jax.ShapeDtypeStruct((k_local - late, full, width), F32),
            jax.ShapeDtypeStruct((n, late, full // n, width), F32),
        ),
        in_specs=[any_spec, vmem, vmem],
        out_specs=(any_spec, any_spec, any_spec),
        scratch_shapes=[
            pltpu.VMEM((tiles, count, rows, LANES), F32),
            pltpu.VMEM((2, count, cols), F32),
            pltpu.VMEM((2, 2, hr, cols), F32),
            pltpu.VMEM((2, hr, cols), F32),
            pltpu.VMEM((2, 2, count, cols), F32),
            pltpu.VMEM((2 * count, cols), BF16),
            pltpu.VMEM((2 * count, cols), BF16),
            pltpu.VMEM((2 * count, 2 * count), BF16),
            pltpu.VMEM((2 * count, 2 * count), BF16),
            pltpu.VMEM((2 * count, 2 * count), BF16),
            pltpu.VMEM((2 * count, 2 * count), BF16),
            dma((chunks, n - 1)), dma((chunks, n - 1)), dma((n, tiles)),
            dma(()), dma((2,)), dma(()), dma((2,)), dma(()), dma((2,)),
            dma((chunks, n - 1)), dma((chunks, n - 1)),
            dma((tiles,)), dma((tiles,)), dma((tiles,)),
        ],
        compiler_params=pltpu.CompilerParams(
            collective_id=0, has_side_effects=True, vmem_limit_bytes=67043328
        ),
        name="born",
    )(x, cosine, sine)


def on_device(green_guess, green_free, retarded, momentum_order):
    n = lax.axis_size("mom")
    k_local, full, width = green_guess.shape[1:]
    count = n * k_local
    fits = n & (n - 1) == 0 and full % (n * SUBLANES) == 0 and lax.axis_size("comp") == 4 and count % 512 == 0 and width % LANES == 0 and k_local % LATE_SHARE == 0
    if not fits:
        return on_device_plain(green_guess, green_free, retarded, momentum_order)
    cosine, sine = small_tables(momentum_order, count, L1)
    _, sigma, late = born_call(n, green_guess[0], cosine, sine, L1)
    pieces = lax.all_to_all(late, "mom", split_axis=0, concat_axis=0, tiled=True)
    green, sigma = dyson_early(sigma, retarded, green_free[0])
    green, sigma = dyson_late(pieces, retarded, green_free[0], green, sigma)
    return green[None], sigma[None]


def solution(mesh):
    return jax.shard_map(
        on_device,
        mesh=mesh,
        in_specs=(
            P("comp", "mom", None, None),
            P("comp", "mom", None, None),
            P("mom", None, None),
            P(),
        ),
        out_specs=(P("comp", "mom", None, None), P("comp", "mom", None, None)),
        check_vma=False,
    )
```

```python
import functools
import math

import jax
import jax.numpy as jnp
from jax import lax
from jax.experimental import pallas as pl
from jax.experimental.pallas import tpu as pltpu
from jax.sharding import PartitionSpec as P

K = 512
L1 = 16


highest = lax.Precision.HIGH


def partner(x, axis, bit):
    return lax.ppermute(x, axis, [(i, i ^ 1 << bit) for i in range(lax.axis_size(axis))])


def phase_tables(momentum_order, count, first_len):
    second_len = count // first_len
    site_ids = jnp.arange(count, dtype=jnp.int32)
    site_one = site_ids // second_len
    site_two = site_ids % second_len
    mom_one = momentum_order // second_len
    mom_two = momentum_order % second_len
    phases = (
        site_one[:, None] * mom_one[None, :] * second_len
        + site_two[:, None] * mom_two[None, :] * first_len
    ) % count
    angles = phases.astype(jnp.float32) * (2.0 * math.pi / count)
    norm_factor = 1.0 / math.sqrt(count)
    return (jnp.cos(angles) * norm_factor, jnp.sin(angles) * norm_factor)


def forward_transform(values, cosine, sine_table, half_width):
    full_shape = values.shape
    flattened = values.reshape(full_shape[0], -1)
    with_cos = jnp.dot(
        cosine, flattened, precision=highest, preferred_element_type=jnp.float32
    ).reshape(full_shape)
    with_sin = jnp.dot(
        sine_table, flattened, precision=highest, preferred_element_type=jnp.float32
    ).reshape(full_shape)
    real_part = with_cos[..., :half_width] - with_sin[..., half_width:]
    imag_part = with_cos[..., half_width:] + with_sin[..., :half_width]
    return jnp.concatenate([real_part, imag_part], axis=-1)


def inverse_transform(values, cos_back, sin_back, half_width):
    full_shape = values.shape
    flattened = values.reshape(full_shape[0], -1)
    with_cos = jnp.dot(
        cos_back, flattened, precision=highest, preferred_element_type=jnp.float32
    ).reshape(full_shape)
    with_sin = jnp.dot(
        sin_back, flattened, precision=highest, preferred_element_type=jnp.float32
    ).reshape(full_shape)
    real_part = with_cos[..., :half_width] + with_sin[..., half_width:]
    imag_part = with_cos[..., half_width:] - with_sin[..., :half_width]
    return jnp.concatenate([real_part, imag_part], axis=-1)


def triple(own_part, second, conj_factor, half_width):
    prod_real = (
        own_part[..., :half_width] * second[..., :half_width]
        - own_part[..., half_width:] * second[..., half_width:]
    )
    prod_imag = (
        own_part[..., :half_width] * second[..., half_width:]
        + own_part[..., half_width:] * second[..., :half_width]
    )
    conj_real = conj_factor[..., :half_width]
    conj_imag = conj_factor[..., half_width:]
    real_part = prod_real * conj_real + prod_imag * conj_imag
    imag_part = prod_imag * conj_real - prod_real * conj_imag
    return -jnp.concatenate([real_part, imag_part], axis=-1)


def dyson(sigma_mom, retarded, free_part, half_width):
    ret_real = retarded[..., :half_width]
    ret_imag = retarded[..., half_width:]
    swapped = jnp.concatenate([-sigma_mom[..., half_width:], sigma_mom[..., :half_width]], axis=-1)
    left_prod = jnp.einsum(
        "kij,kjx->kix", ret_real, sigma_mom, precision=highest, preferred_element_type=jnp.float32
    )
    left_prod = left_prod + jnp.einsum(
        "kij,kjx->kix", ret_imag, swapped, precision=highest, preferred_element_type=jnp.float32
    )
    turned = jnp.concatenate([left_prod[..., half_width:], -left_prod[..., :half_width]], axis=-1)
    real_part = jnp.einsum(
        "kim,kjm->kij", left_prod, retarded, precision=highest, preferred_element_type=jnp.float32
    )
    imag_part = jnp.einsum(
        "kim,kjm->kij", turned, retarded, precision=highest, preferred_element_type=jnp.float32
    )
    return free_part + jnp.concatenate([real_part, imag_part], axis=-1)


CHUNKS = 3
GROUPS = 4


def exchange(send, axis):
    size = lax.axis_size(axis)
    return [send[0]] + [
        lax.ppermute(send[s], axis, [(i, i ^ s) for i in range(size)]) for s in range(1, size)
    ]


def on_device_plain(green_guess, green_free, retarded, momentum_order):
    mom_count = lax.axis_size("mom")
    me = lax.axis_index("mom")
    width = green_guess.shape[-1]
    half_width = width // 2
    k_local = green_guess.shape[1]
    tile_rows = half_width // mom_count
    rows = tile_rows // CHUNKS
    group = k_local // GROUPS
    cosine, sine_table = phase_tables(momentum_order, K, L1)
    cos_back = cosine.T
    sin_back = sine_table.T
    free_local = green_free[0]
    current = green_guess[0]

    tiled = current.reshape(k_local, mom_count, CHUNKS, rows, width)
    arrived = [
        lax.all_to_all(tiled[:, :, c], "mom", split_axis=1, concat_axis=0, tiled=True)
        for c in range(CHUNKS)
    ]
    pieces = []
    for c in range(CHUNKS):
        in_sites = forward_transform(arrived[c][:, 0], cosine, sine_table, half_width)
        spin_other = partner(in_sites, "comp", 1)
        cross_other = partner(spin_other, "comp", 0)
        sigma_sites = triple(in_sites, spin_other, cross_other, half_width)
        tile = inverse_transform(sigma_sites, cos_back, sin_back, half_width)
        pieces.append(lax.all_to_all(tile.reshape(mom_count, k_local, 1, rows, width), "mom", split_axis=0, concat_axis=2, tiled=True))
    sigma = jnp.stack(pieces, axis=3).reshape(k_local, half_width, width)
    return (dyson(sigma, retarded, free_local, half_width)[None], sigma[None])


BF16 = jnp.bfloat16
F32 = jnp.float32
SUBLANES = 8
LANES = 128
LATE_SHARE = 8
LATE_VMEM = 36 << 20
MESH = pl.DeviceIdType.MESH


def flip(index, mask, count):
    out, bit = 0, 1
    while bit < count:
        part, turn = lax.rem(lax.div(index, bit), 2), lax.rem(lax.div(mask, bit), 2)
        out = out + bit * (part + turn - 2 * part * turn)
        bit *= 2
    return out


def send_orders(count):
    up, half = [], count // 2
    while half:
        up += range(half, 2 * half)
        half //= 2
    return up, list(range(count - 1, 0, -1))


def split(value):
    high = value.astype(BF16)
    return high, (value - high.astype(F32)).astype(BF16)


def mm(left, right, dims=((1,), (0,))):
    return lax.dot_general(left, right, (dims, ((), ())), preferred_element_type=F32)


def mm3(left, right, dims=((1,), (0,))):
    return mm(left[0], right[0], dims) + (mm(left[0], right[1], dims) + mm(left[1], right[0], dims))


def small_tables(order, count, first_len):
    second_len = count // first_len
    shift = second_len.bit_length() - 1
    ids = lax.broadcasted_iota(jnp.int32, (first_len + second_len, count), 0)
    one = lax.shift_right_logical(order, jnp.full_like(order, shift))
    two = order & (second_len - 1)
    phases = jnp.where(
        ids < first_len, ids * one * second_len, (ids - first_len) * two * first_len
    ) & (count - 1)
    angles = phases.astype(F32) * (2.0 * math.pi / count)
    scale = jnp.where(ids < first_len, 1.0 / math.sqrt(count), 1.0).astype(F32)
    return jnp.cos(angles) * scale, jnp.sin(angles) * scale


def stacked(left, right, dims=((1,), (0,))):
    size = left[0].shape[0]
    both = mm(jnp.concatenate(left, axis=0), right[0], dims)
    return both[:size] + (both[size:] + mm(left[0], right[1], dims))


def dyson_block(sigma, ret, free):
    half = sigma.shape[0]
    lane = lax.broadcasted_iota(jnp.int32, sigma.shape, 1)
    sign = jnp.where(lane < half, -1.0, 1.0).astype(F32)
    ret_parts = split(ret)
    sig_pair = [jnp.concatenate(p, axis=0) for p in zip(split(sigma), split(pltpu.roll(sigma, half, 1) * sign))]
    ret_pair = [jnp.concatenate(p, axis=0) for p in zip(ret_parts, split(pltpu.roll(ret, half, 1) * sign))]
    left = stacked(ret_parts, sig_pair)
    return free + stacked(split(left), ret_pair, ((1,), (1,)))


def dyson_early_kernel(sig_ref, ret_ref, free_ref, green_ref, out_ref):
    for i in range(sig_ref.shape[0]):
        sigma = sig_ref[i]
        out_ref[i] = sigma
        green_ref[i] = dyson_block(sigma, ret_ref[i], free_ref[i])


def dyson_late_kernel(sig_ref, ret_ref, free_ref, _green, _out, green_ref, out_ref):
    step = ret_ref.shape[0]
    for i in range(step):
        sigma = sig_ref[:, pl.program_id(0) * step + i].reshape(ret_ref.shape[1:])
        out_ref[i] = sigma
        green_ref[i] = dyson_block(sigma, ret_ref[i], free_ref[i])


def dyson_cost(count, half):
    return pl.CostEstimate(
        flops=count * half * half * half * 8 * 6, bytes_accessed=count * half * half * 2 * 4 * 5, transcendentals=0)


def dyson_early(sigma, retarded, free):
    early, half, width = sigma.shape
    step = math.gcd(early, 4)
    spec = pl.BlockSpec((step, half, width), lambda k: (k, 0, 0))
    shape = jax.ShapeDtypeStruct(free.shape, F32)
    return pl.pallas_call(
        dyson_early_kernel,
        grid=(early // step,),
        in_specs=[spec] * 3,
        out_specs=(spec, spec),
        out_shape=(shape, shape),
        cost_estimate=dyson_cost(early, half),
        name="dyson_early",
    )(sigma, retarded, free)


def dyson_late(pieces, retarded, free, green, sigma):
    late = pieces.shape[1]
    k_local, half, width = free.shape
    early = k_local - late
    step = math.gcd(math.gcd(early, late), 2)
    spec = pl.BlockSpec((step, half, width), lambda k: (early // step + k, 0, 0))
    any_spec = pl.BlockSpec(memory_space=pl.ANY)
    shape = jax.ShapeDtypeStruct(free.shape, F32)
    pieces = pltpu.with_memory_space_constraint(pieces, pltpu.VMEM)
    return pl.pallas_call(
        dyson_late_kernel,
        grid=(late // step,),
        in_specs=[pl.BlockSpec(memory_space=pltpu.VMEM), spec, spec, any_spec, any_spec],
        out_specs=(spec, spec),
        out_shape=(shape, shape),
        input_output_aliases={3: 0, 4: 1},
        cost_estimate=dyson_cost(late, half),
        compiler_params=pltpu.CompilerParams(vmem_limit_bytes=LATE_VMEM),
        name="dyson_late",
    )(pieces, retarded, free, green, sigma)


def born_kernel(
    n, chunks, first_len,
    x_hbm, order_ref,
    recv_hbm, sig_hbm, late_hbm,
    cos_ref, sin_ref, buf, site, gs, qsend, q, zhi, zlo, fwd_hi, fwd_lo, inv_hi, inv_lo,
    fwd_send, fwd_recv, load_sem, gs_send, gs_recv, q_send, q_recv, rel_send, rel_recv, ret_send, ret_recv, own_sem, stage_sem, late_sem,
):
    me = lax.axis_index("mom")
    comp = lax.axis_index("comp")
    core = lax.rem(comp, 2)
    sibling = {"comp": comp + 1 - 2 * core}
    across = {"comp": lax.rem(comp + 2, 4)}
    sgn = (1 - 2 * core).astype(F32)
    k_local, full, width = x_hbm.shape
    half = width // 2
    count = n * k_local
    rows = SUBLANES
    pairs = rows // 2
    cols = pairs * width
    second_len = count // first_len
    early = sig_hbm.shape[0]
    late = k_local - early
    peers = [flip(me, a + core * (b - a), n) for a, b in zip(*send_orders(n))]
    hr = count // 2

    barrier = pltpu.get_barrier_semaphore()
    for peer in peers:
        pl.semaphore_signal(barrier, inc=1, device_id={"mom": peer}, device_id_type=MESH)
    pl.semaphore_signal(barrier, inc=1, device_id=sibling, device_id_type=MESH)
    pl.semaphore_signal(barrier, inc=1, device_id=across, device_id_type=MESH)
    pl.semaphore_wait(barrier, len(peers) + 2)

    def row_of(device, c):
        return pl.multiple_of((device * chunks + c) * rows, rows)

    def fwd_copy(c, i):
        return pltpu.make_async_remote_copy(
            src_ref=x_hbm.at[:, pl.ds(row_of(peers[i], c), rows), :],
            dst_ref=recv_hbm.at[c, pl.ds(me * k_local, k_local)],
            send_sem=fwd_send.at[c, i], recv_sem=fwd_recv.at[c, i],
            device_id={"mom": peers[i]}, device_id_type=MESH)

    def ret_copy(c, i):
        return pltpu.make_async_remote_copy(
            src_ref=recv_hbm.at[c, pl.ds(peers[i] * k_local, early)],
            dst_ref=sig_hbm.at[:, pl.ds(row_of(me, c), rows), :],
            send_sem=ret_send.at[c, i], recv_sem=ret_recv.at[c, i],
            device_id={"mom": peers[i]}, device_id_type=MESH)

    def send_forward(c, carry):
        for i in range(len(peers)):
            fwd_copy(c, i).start()
        return carry

    lax.fori_loop(0, chunks, send_forward, 0)

    cos_ref[...], sin_ref[...] = small_tables(order_ref[...], count, first_len)

    def build(one, carry):
        c1 = cos_ref[pl.ds(one, 1), :]
        s1 = sin_ref[pl.ds(one, 1), :]
        c2 = cos_ref[pl.ds(first_len, second_len), :]
        s2 = sin_ref[pl.ds(first_len, second_len), :]
        at = pl.ds(pl.multiple_of(one * second_len, second_len), second_len)
        low = pl.ds(pl.multiple_of(count + one * second_len, second_len), second_len)
        cosine = c1 * c2 - s1 * s2
        sine = s1 * c2 + c1 * s2
        site[0, at, 0:count] = cosine
        site[1, at, 0:count] = sine
        ch, cl = split(cosine)
        sh, sl = split(sine)
        for ref, cv, sv in ((fwd_hi, ch, sh), (fwd_lo, cl, sl)):
            ref[at, 0:count] = cv
            ref[at, count:2 * count] = -sv
            ref[low, 0:count] = sv
            ref[low, count:2 * count] = cv
        return carry

    lax.fori_loop(0, first_len, build, 0)

    def turn(b, carry):
        at = pl.ds(pl.multiple_of(b * 128, 128), 128)
        low = pl.ds(pl.multiple_of(count + b * 128, 128), 128)
        ch, cl = split(site[0, :, at].T)
        sh, sl = split(site[1, :, at].T)
        for ref, cv, sv in ((inv_hi, ch, sh), (inv_lo, cl, sl)):
            ref[at, 0:count] = cv
            ref[at, count:2 * count] = sv
            ref[low, 0:count] = -sv
            ref[low, count:2 * count] = cv
        return carry

    lax.fori_loop(0, count // 128, turn, 0)

    tiles = width // LANES
    flat = buf.reshape(tiles, count * rows, LANES)
    by_owner = buf.reshape(tiles, n, k_local, rows, LANES)

    def take(start, size):
        return jnp.concatenate([flat[j, pl.ds(start, size, stride=rows), :] for j in range(tiles)], axis=1)

    def put(start, size, value):
        for j in range(tiles):
            flat[j, pl.ds(start, size, stride=rows), :] = value[:, j * LANES:(j + 1) * LANES]

    def lanes_of(j):
        return pl.ds(j * LANES, LANES)


    def chunk_step(c, carry):
        slot = lax.rem(c, 2)
        loads = []
        for j in range(tiles):
            loads.append(pltpu.make_async_copy(
                x_hbm.at[:, pl.ds(row_of(me, c), rows), lanes_of(j)],
                buf.at[j, pl.ds(me * k_local, k_local)], load_sem.at[n - 1, j]))
            loads[-1].start()
        for i in range(len(peers)):
            fwd_copy(c, i).wait_recv()
            at = pl.ds(peers[i] * k_local, k_local)
            for j in range(tiles):
                loads.append(pltpu.make_async_copy(
                    recv_hbm.at[c, at, :, lanes_of(j)], buf.at[j, at], load_sem.at[i, j]))
                loads[-1].start()
        for load in loads:
            load.wait()

        kb = k_local

        def stage(b, carry):
            lane = lax.broadcasted_iota(jnp.int32, (kb, width), 1)
            at = pl.ds(pl.multiple_of(b * kb, kb), kb)
            low = pl.ds(pl.multiple_of(count + b * kb, kb), kb)
            for p in range(pairs):
                r0 = take(b * (kb * rows) + 2 * p, kb)
                r1 = take(b * (kb * rows) + 2 * p + 1, kb)
                re = jnp.where(lane < half, r0, pltpu.roll(r1, half, 1))
                im = jnp.where(lane < half, pltpu.roll(r0, half, 1), r1)
                here = pl.ds(p * width, width)
                rh, rl = split(re)
                ih, il = split(im)
                zhi[at, here] = rh
                zlo[at, here] = rl
                zhi[low, here] = ih
                zlo[low, here] = il
            return carry

        lax.fori_loop(0, count // kb, stage, 0)

        def forward(step, carry):
            m, t = lax.div(step, 3), lax.rem(step, 3)
            plane, part = lax.div(m, 2), lax.rem(m, 2)
            left = pl.ds(pl.multiple_of(m * hr, hr), hr)
            right = pl.ds(pl.multiple_of(t * (cols // 3), cols // 3), cols // 3)
            value = mm3((fwd_hi[left, :], fwd_lo[left, :]), (zhi[:, right], zlo[:, right]))
            site[plane, pl.ds(pl.multiple_of(part * hr, hr), hr), right] = value
            return carry

        lax.fori_loop(0, 12, forward, 0)

        mine = pl.multiple_of(core * hr, hr)
        other = pl.multiple_of((1 - core) * hr, hr)
        gs_copy = pltpu.make_async_remote_copy(
            src_ref=site.at[:, pl.ds(other, hr), :], dst_ref=gs.at[slot],
            send_sem=gs_send, recv_sem=gs_recv.at[slot], device_id=sibling, device_id_type=MESH)
        gs_copy.start()
        gs_copy.wait_recv()

        rb = 16

        def pair(b, carry):
            here = pl.ds(pl.multiple_of(b * rb, rb), rb)
            at = pl.ds(pl.multiple_of(mine + b * rb, rb), rb)
            ore, oim = site[0, at, :], site[1, at, :]
            sre, sim = gs[slot, 0, here, :], gs[slot, 1, here, :]
            qsend[0, here, :] = ore * sre + oim * sim
            qsend[1, here, :] = sgn * (oim * sre - ore * sim)
            return carry

        lax.fori_loop(0, hr // rb, pair, 0)

        q_copy = pltpu.make_async_remote_copy(
            src_ref=qsend, dst_ref=q.at[slot, :, pl.ds(mine, hr), :],
            send_sem=q_send, recv_sem=q_recv.at[slot], device_id=across, device_id_type=MESH)
        q_copy.start()
        q_copy.wait_recv()
        relay = pltpu.make_async_remote_copy(
            src_ref=q.at[slot, :, pl.ds(mine, hr), :], dst_ref=q.at[slot, :, pl.ds(mine, hr), :],
            send_sem=rel_send, recv_sem=rel_recv.at[slot], device_id=sibling, device_id_type=MESH)
        relay.start()

        def sigma_rows(base):
            def body(b, carry):
                at = pl.ds(pl.multiple_of(base + b * rb, rb), rb)
                low = pl.ds(pl.multiple_of(count + base + b * rb, rb), rb)
                gre, gim = site[0, at, :], site[1, at, :]
                qre, qim = q[slot, 0, at, :], sgn * q[slot, 1, at, :]
                rh, rl = split(gim * qim - gre * qre)
                ih, il = split(-(gre * qim + gim * qre))
                zhi[at, :] = rh
                zlo[at, :] = rl
                zhi[low, :] = ih
                zlo[low, :] = il
                return carry

            lax.fori_loop(0, hr // rb, body, 0)

        sigma_rows(mine)
        relay.wait_recv()
        sigma_rows(other)

        def inverse(step, carry):
            m, t = lax.div(step, 2), lax.rem(step, 2)
            top = pl.ds(pl.multiple_of(m * hr, hr), hr)
            bot = pl.ds(pl.multiple_of(count + m * hr, hr), hr)
            right = pl.ds(pl.multiple_of(t * (2 * width), 2 * width), 2 * width)
            z = (zhi[:, right], zlo[:, right])
            re = mm3((inv_hi[top, :], inv_lo[top, :]), z)
            im = mm3((inv_hi[bot, :], inv_lo[bot, :]), z)
            lane = lax.broadcasted_iota(jnp.int32, (hr, width), 1)
            for p in range(2):
                rep = re[:, p * width:(p + 1) * width]
                imp = im[:, p * width:(p + 1) * width]
                r0 = jnp.where(lane < half, rep, pltpu.roll(imp, half, 1))
                r1 = jnp.where(lane < half, pltpu.roll(rep, half, 1), imp)
                base = m * (hr * rows) + t * 4 + 2 * p
                put(base, hr, r0)
                put(base + 1, hr, r1)
            return carry

        lax.fori_loop(0, 4, inverse, 0)

        outs = []
        for j in range(tiles):
            outs.append(pltpu.make_async_copy(buf.at[j], recv_hbm.at[c, :, :, lanes_of(j)], stage_sem.at[j]))
            outs.append(pltpu.make_async_copy(
                buf.at[j, pl.ds(me * k_local, early)],
                sig_hbm.at[:, pl.ds(row_of(me, c), rows), lanes_of(j)], own_sem.at[j]))
            outs.append(pltpu.make_async_copy(
                by_owner.at[j, :, pl.ds(early, late)],
                late_hbm.at[:, :, pl.ds(pl.multiple_of(c * rows, rows), rows), lanes_of(j)], late_sem.at[j]))
        for out in outs:
            out.start()
        for out in outs:
            out.wait()

        for i in range(len(peers)):
            ret_copy(c, i).start()
        gs_copy.wait_send()
        q_copy.wait_send()
        relay.wait_send()
        return carry

    lax.fori_loop(0, chunks, chunk_step, 0)

    def finish(c, carry):
        for i in range(len(peers)):
            fwd_copy(c, i).wait_send()
            ret_copy(c, i).wait()
        return carry

    lax.fori_loop(0, chunks, finish, 0)


def born_call(n, x, order, first_len):
    k_local, full, width = x.shape
    count = n * k_local
    rows = SUBLANES
    chunks = full // n // rows
    cols = rows * width // 2
    tiles = width // LANES
    hr = count // 2
    late = k_local // LATE_SHARE
    any_spec = pl.BlockSpec(memory_space=pl.ANY)
    vmem = pl.BlockSpec(memory_space=pltpu.VMEM)
    dma = pltpu.SemaphoreType.DMA
    return pl.pallas_call(
        functools.partial(born_kernel, n, chunks, first_len),
        out_shape=(
            jax.ShapeDtypeStruct((chunks, count, rows, width), F32),
            jax.ShapeDtypeStruct((k_local - late, full, width), F32),
            jax.ShapeDtypeStruct((n, late, full // n, width), F32),
        ),
        in_specs=[any_spec, vmem],
        out_specs=(any_spec, any_spec, any_spec),
        scratch_shapes=[
            pltpu.VMEM((first_len + count // first_len, count), F32),
            pltpu.VMEM((first_len + count // first_len, count), F32),
            pltpu.VMEM((tiles, count, rows, LANES), F32),
            pltpu.VMEM((2, count, cols), F32),
            pltpu.VMEM((2, 2, hr, cols), F32),
            pltpu.VMEM((2, hr, cols), F32),
            pltpu.VMEM((2, 2, count, cols), F32),
            pltpu.VMEM((2 * count, cols), BF16),
            pltpu.VMEM((2 * count, cols), BF16),
            pltpu.VMEM((2 * count, 2 * count), BF16),
            pltpu.VMEM((2 * count, 2 * count), BF16),
            pltpu.VMEM((2 * count, 2 * count), BF16),
            pltpu.VMEM((2 * count, 2 * count), BF16),
            dma((chunks, n - 1)), dma((chunks, n - 1)), dma((n, tiles)),
            dma(()), dma((2,)), dma(()), dma((2,)), dma(()), dma((2,)),
            dma((chunks, n - 1)), dma((chunks, n - 1)),
            dma((tiles,)), dma((tiles,)), dma((tiles,)),
        ],
        compiler_params=pltpu.CompilerParams(
            collective_id=0, has_side_effects=True, vmem_limit_bytes=67043328
        ),
        name="born",
    )(x, order)


def on_device(green_guess, green_free, retarded, momentum_order):
    n = lax.axis_size("mom")
    k_local, full, width = green_guess.shape[1:]
    count = n * k_local
    fits = n & (n - 1) == 0 and count & (count - 1) == 0 and full % (n * SUBLANES) == 0 and lax.axis_size("comp") == 4 and count % 512 == 0 and width % LANES == 0 and k_local % LATE_SHARE == 0
    if not fits:
        return on_device_plain(green_guess, green_free, retarded, momentum_order)
    _, sigma, late = born_call(n, green_guess[0], momentum_order.astype(jnp.int32)[None], L1)
    pieces = lax.all_to_all(late, "mom", split_axis=0, concat_axis=0, tiled=True)
    green, sigma = dyson_early(sigma, retarded, green_free[0])
    green, sigma = dyson_late(pieces, retarded, green_free[0], green, sigma)
    return green[None], sigma[None]


def solution(mesh):
    return jax.shard_map(
        on_device,
        mesh=mesh,
        in_specs=(
            P("comp", "mom", None, None),
            P("comp", "mom", None, None),
            P("mom", None, None),
            P(),
        ),
        out_specs=(P("comp", "mom", None, None), P("comp", "mom", None, None)),
        check_vma=False,
    )
```

```python
import functools
import math

import jax
import jax.numpy as jnp
from jax import lax
from jax.experimental import pallas as pl
from jax.experimental.pallas import tpu as pltpu
from jax.sharding import PartitionSpec as P

K = 512
L1 = 16


highest = lax.Precision.HIGH


def partner(x, axis, bit):
    return lax.ppermute(x, axis, [(i, i ^ 1 << bit) for i in range(lax.axis_size(axis))])


def phase_tables(momentum_order, count, first_len):
    second_len = count // first_len
    site_ids = jnp.arange(count, dtype=jnp.int32)
    site_one = site_ids // second_len
    site_two = site_ids % second_len
    mom_one = momentum_order // second_len
    mom_two = momentum_order % second_len
    phases = (
        site_one[:, None] * mom_one[None, :] * second_len
        + site_two[:, None] * mom_two[None, :] * first_len
    ) % count
    angles = phases.astype(jnp.float32) * (2.0 * math.pi / count)
    norm_factor = 1.0 / math.sqrt(count)
    return (jnp.cos(angles) * norm_factor, jnp.sin(angles) * norm_factor)


def forward_transform(values, cosine, sine_table, half_width):
    full_shape = values.shape
    flattened = values.reshape(full_shape[0], -1)
    with_cos = jnp.dot(
        cosine, flattened, precision=highest, preferred_element_type=jnp.float32
    ).reshape(full_shape)
    with_sin = jnp.dot(
        sine_table, flattened, precision=highest, preferred_element_type=jnp.float32
    ).reshape(full_shape)
    real_part = with_cos[..., :half_width] - with_sin[..., half_width:]
    imag_part = with_cos[..., half_width:] + with_sin[..., :half_width]
    return jnp.concatenate([real_part, imag_part], axis=-1)


def inverse_transform(values, cos_back, sin_back, half_width):
    full_shape = values.shape
    flattened = values.reshape(full_shape[0], -1)
    with_cos = jnp.dot(
        cos_back, flattened, precision=highest, preferred_element_type=jnp.float32
    ).reshape(full_shape)
    with_sin = jnp.dot(
        sin_back, flattened, precision=highest, preferred_element_type=jnp.float32
    ).reshape(full_shape)
    real_part = with_cos[..., :half_width] + with_sin[..., half_width:]
    imag_part = with_cos[..., half_width:] - with_sin[..., :half_width]
    return jnp.concatenate([real_part, imag_part], axis=-1)


def triple(own_part, second, conj_factor, half_width):
    prod_real = (
        own_part[..., :half_width] * second[..., :half_width]
        - own_part[..., half_width:] * second[..., half_width:]
    )
    prod_imag = (
        own_part[..., :half_width] * second[..., half_width:]
        + own_part[..., half_width:] * second[..., :half_width]
    )
    conj_real = conj_factor[..., :half_width]
    conj_imag = conj_factor[..., half_width:]
    real_part = prod_real * conj_real + prod_imag * conj_imag
    imag_part = prod_imag * conj_real - prod_real * conj_imag
    return -jnp.concatenate([real_part, imag_part], axis=-1)


def dyson(sigma_mom, retarded, free_part, half_width):
    ret_real = retarded[..., :half_width]
    ret_imag = retarded[..., half_width:]
    swapped = jnp.concatenate([-sigma_mom[..., half_width:], sigma_mom[..., :half_width]], axis=-1)
    left_prod = jnp.einsum(
        "kij,kjx->kix", ret_real, sigma_mom, precision=highest, preferred_element_type=jnp.float32
    )
    left_prod = left_prod + jnp.einsum(
        "kij,kjx->kix", ret_imag, swapped, precision=highest, preferred_element_type=jnp.float32
    )
    turned = jnp.concatenate([left_prod[..., half_width:], -left_prod[..., :half_width]], axis=-1)
    real_part = jnp.einsum(
        "kim,kjm->kij", left_prod, retarded, precision=highest, preferred_element_type=jnp.float32
    )
    imag_part = jnp.einsum(
        "kim,kjm->kij", turned, retarded, precision=highest, preferred_element_type=jnp.float32
    )
    return free_part + jnp.concatenate([real_part, imag_part], axis=-1)


CHUNKS = 3
GROUPS = 4


def exchange(send, axis):
    size = lax.axis_size(axis)
    return [send[0]] + [
        lax.ppermute(send[s], axis, [(i, i ^ s) for i in range(size)]) for s in range(1, size)
    ]


def on_device_plain(green_guess, green_free, retarded, momentum_order):
    mom_count = lax.axis_size("mom")
    me = lax.axis_index("mom")
    width = green_guess.shape[-1]
    half_width = width // 2
    k_local = green_guess.shape[1]
    tile_rows = half_width // mom_count
    rows = tile_rows // CHUNKS
    group = k_local // GROUPS
    cosine, sine_table = phase_tables(momentum_order, K, L1)
    cos_back = cosine.T
    sin_back = sine_table.T
    free_local = green_free[0]
    current = green_guess[0]

    tiled = current.reshape(k_local, mom_count, CHUNKS, rows, width)
    arrived = [
        lax.all_to_all(tiled[:, :, c], "mom", split_axis=1, concat_axis=0, tiled=True)
        for c in range(CHUNKS)
    ]
    pieces = []
    for c in range(CHUNKS):
        in_sites = forward_transform(arrived[c][:, 0], cosine, sine_table, half_width)
        spin_other = partner(in_sites, "comp", 1)
        cross_other = partner(spin_other, "comp", 0)
        sigma_sites = triple(in_sites, spin_other, cross_other, half_width)
        tile = inverse_transform(sigma_sites, cos_back, sin_back, half_width)
        pieces.append(lax.all_to_all(tile.reshape(mom_count, k_local, 1, rows, width), "mom", split_axis=0, concat_axis=2, tiled=True))
    sigma = jnp.stack(pieces, axis=3).reshape(k_local, half_width, width)
    return (dyson(sigma, retarded, free_local, half_width)[None], sigma[None])


BF16 = jnp.bfloat16
F32 = jnp.float32
SUBLANES = 8
LANES = 128
LATE_SHARE = 8
LATE_VMEM = 36 << 20
MESH = pl.DeviceIdType.MESH


def flip(index, mask, count):
    out, bit = 0, 1
    while bit < count:
        part, turn = lax.rem(lax.div(index, bit), 2), lax.rem(lax.div(mask, bit), 2)
        out = out + bit * (part + turn - 2 * part * turn)
        bit *= 2
    return out


def send_orders(count):
    up, half = [], count // 2
    while half:
        up += range(half, 2 * half)
        half //= 2
    return up, list(range(count - 1, 0, -1))


def peers_of(me, n):
    core = lax.rem(lax.axis_index("comp"), 2)
    return [flip(me, a + core * (b - a), n) for a, b in zip(*send_orders(n))]


def send_late(blocks, n):
    got = []
    for block, masks in zip(blocks, zip(*send_orders(n))):
        pairs = [(c * n + m, c * n + (m ^ masks[c % 2])) for c in range(lax.axis_size("comp")) for m in range(n)]
        got.append(lax.ppermute(block, ("comp", "mom"), pairs))
    return got + [blocks[-1]]


def split(value):
    high = value.astype(BF16)
    return high, (value - high.astype(F32)).astype(BF16)


def mm(left, right, dims=((1,), (0,))):
    return lax.dot_general(left, right, (dims, ((), ())), preferred_element_type=F32)


def mm3(left, right, dims=((1,), (0,))):
    return mm(left[0], right[0], dims) + (mm(left[0], right[1], dims) + mm(left[1], right[0], dims))


def small_tables(order, count, first_len):
    second_len = count // first_len
    shift = second_len.bit_length() - 1
    ids = lax.broadcasted_iota(jnp.int32, (first_len + second_len, count), 0)
    one = lax.shift_right_logical(order, jnp.full_like(order, shift))
    two = order & (second_len - 1)
    phases = jnp.where(
        ids < first_len, ids * one * second_len, (ids - first_len) * two * first_len
    ) & (count - 1)
    angles = phases.astype(F32) * (2.0 * math.pi / count)
    scale = jnp.where(ids < first_len, 1.0 / math.sqrt(count), 1.0).astype(F32)
    return jnp.cos(angles) * scale, jnp.sin(angles) * scale


def stacked(left, right, dims=((1,), (0,))):
    size = left[0].shape[0]
    both = mm(jnp.concatenate(left, axis=0), right[0], dims)
    return both[:size] + (both[size:] + mm(left[0], right[1], dims))


def dyson_block(sigma, ret, free):
    half = sigma.shape[0]
    lane = lax.broadcasted_iota(jnp.int32, sigma.shape, 1)
    sign = jnp.where(lane < half, -1.0, 1.0).astype(F32)
    ret_parts = split(ret)
    sig_pair = [jnp.concatenate(p, axis=0) for p in zip(split(sigma), split(pltpu.roll(sigma, half, 1) * sign))]
    ret_pair = [jnp.concatenate(p, axis=0) for p in zip(ret_parts, split(pltpu.roll(ret, half, 1) * sign))]
    left = stacked(ret_parts, sig_pair)
    return free + stacked(split(left), ret_pair, ((1,), (1,)))


def dyson_early_kernel(sig_ref, ret_ref, free_ref, green_ref, out_ref):
    for i in range(sig_ref.shape[0]):
        sigma = sig_ref[i]
        out_ref[i] = sigma
        green_ref[i] = dyson_block(sigma, ret_ref[i], free_ref[i])


def dyson_late_kernel(n, early, *refs):
    pieces, (ret_hbm, free_hbm, _, _, green_hbm, out_hbm) = refs[:n], refs[n:n + 6]
    sig, ret, free, green, ret_sem, free_sem, green_sem, out_sem = refs[n + 6:]
    late = sig.shape[0]
    tile = sig.shape[1] // n
    loads, stores = [], []
    for k in range(late):
        loads.append((
            pltpu.make_async_copy(ret_hbm.at[early + k], ret.at[k], ret_sem.at[k]),
            pltpu.make_async_copy(free_hbm.at[early + k], free.at[k], free_sem.at[k])))
        stores.append((
            pltpu.make_async_copy(sig.at[k], out_hbm.at[early + k], out_sem.at[k]),
            pltpu.make_async_copy(green.at[k], green_hbm.at[early + k], green_sem.at[k])))
    for pair in loads:
        for load in pair:
            load.start()
    me = lax.axis_index("mom")
    owners = peers_of(me, n) + [me]
    for k in range(late):
        for piece, owner in zip(pieces, owners):
            sig[k, pl.ds(pl.multiple_of(owner * tile, SUBLANES), tile), :] = piece[k]
        stores[k][0].start()
    for k in range(late):
        for load in loads[k]:
            load.wait()
        green[k] = dyson_block(sig[k], ret[k], free[k])
        stores[k][1].start()
    for pair in stores:
        for store in pair:
            store.wait()


def dyson_cost(count, half):
    return pl.CostEstimate(
        flops=count * half * half * half * 8 * 6, bytes_accessed=count * half * half * 2 * 4 * 5, transcendentals=0)


def dyson_early(sigma, retarded, free):
    early, half, width = sigma.shape
    step = math.gcd(early, 4)
    spec = pl.BlockSpec((step, half, width), lambda k: (k, 0, 0))
    shape = jax.ShapeDtypeStruct(free.shape, F32)
    return pl.pallas_call(
        dyson_early_kernel,
        grid=(early // step,),
        in_specs=[spec] * 3,
        out_specs=(spec, spec),
        out_shape=(shape, shape),
        cost_estimate=dyson_cost(early, half),
        name="dyson_early",
    )(sigma, retarded, free)


def dyson_late(pieces, retarded, free, green, sigma):
    n, late = len(pieces), pieces[0].shape[0]
    k_local, half, width = free.shape
    any_spec = pl.BlockSpec(memory_space=pl.ANY)
    vmem = pl.BlockSpec(memory_space=pltpu.VMEM)
    shape = jax.ShapeDtypeStruct(free.shape, F32)
    return pl.pallas_call(
        functools.partial(dyson_late_kernel, n, k_local - late),
        in_specs=[vmem] * n + [any_spec] * 4,
        out_specs=(any_spec, any_spec),
        out_shape=(shape, shape),
        scratch_shapes=[pltpu.VMEM((late, half, width), F32)] * 4 + [pltpu.SemaphoreType.DMA((late,))] * 4,
        input_output_aliases={n + 2: 0, n + 3: 1},
        cost_estimate=dyson_cost(late, half),
        compiler_params=pltpu.CompilerParams(vmem_limit_bytes=LATE_VMEM),
        name="dyson_late",
    )(*pieces, retarded, free, green, sigma)


def born_kernel(
    n, chunks, first_len,
    x_hbm, order_ref,
    recv_hbm, sig_hbm, *rest,
):
    late_hbm = rest[:n]
    (cos_ref, sin_ref, buf, site, gs, qsend, q, zhi, zlo, fwd_hi, fwd_lo, inv_hi, inv_lo,
     fwd_send, fwd_recv, load_sem, gs_send, gs_recv, q_send, q_recv, rel_send, rel_recv,
     ret_send, ret_recv, own_sem, stage_sem, late_sem) = rest[n:]
    me = lax.axis_index("mom")
    comp = lax.axis_index("comp")
    core = lax.rem(comp, 2)
    sibling = {"comp": comp + 1 - 2 * core}
    across = {"comp": lax.rem(comp + 2, 4)}
    sgn = (1 - 2 * core).astype(F32)
    k_local, full, width = x_hbm.shape
    half = width // 2
    count = n * k_local
    rows = SUBLANES
    pairs = rows // 2
    cols = pairs * width
    second_len = count // first_len
    early = sig_hbm.shape[0]
    late = k_local - early
    peers = peers_of(me, n)
    hr = count // 2

    barrier = pltpu.get_barrier_semaphore()
    for peer in peers:
        pl.semaphore_signal(barrier, inc=1, device_id={"mom": peer}, device_id_type=MESH)
    pl.semaphore_signal(barrier, inc=1, device_id=sibling, device_id_type=MESH)
    pl.semaphore_signal(barrier, inc=1, device_id=across, device_id_type=MESH)
    pl.semaphore_wait(barrier, len(peers) + 2)

    def row_of(device, c):
        return pl.multiple_of((device * chunks + c) * rows, rows)

    def fwd_copy(c, i):
        return pltpu.make_async_remote_copy(
            src_ref=x_hbm.at[:, pl.ds(row_of(peers[i], c), rows), :],
            dst_ref=recv_hbm.at[c, pl.ds(me * k_local, k_local)],
            send_sem=fwd_send.at[c, i], recv_sem=fwd_recv.at[c, i],
            device_id={"mom": peers[i]}, device_id_type=MESH)

    def ret_copy(c, i):
        return pltpu.make_async_remote_copy(
            src_ref=recv_hbm.at[c, pl.ds(peers[i] * k_local, early)],
            dst_ref=sig_hbm.at[:, pl.ds(row_of(me, c), rows), :],
            send_sem=ret_send.at[c, i], recv_sem=ret_recv.at[c, i],
            device_id={"mom": peers[i]}, device_id_type=MESH)

    def send_forward(c, carry):
        for i in range(len(peers)):
            fwd_copy(c, i).start()
        return carry

    lax.fori_loop(0, chunks, send_forward, 0)

    cos_ref[...], sin_ref[...] = small_tables(order_ref[...], count, first_len)

    def build(one, carry):
        c1 = cos_ref[pl.ds(one, 1), :]
        s1 = sin_ref[pl.ds(one, 1), :]
        c2 = cos_ref[pl.ds(first_len, second_len), :]
        s2 = sin_ref[pl.ds(first_len, second_len), :]
        at = pl.ds(pl.multiple_of(one * second_len, second_len), second_len)
        low = pl.ds(pl.multiple_of(count + one * second_len, second_len), second_len)
        cosine = c1 * c2 - s1 * s2
        sine = s1 * c2 + c1 * s2
        site[0, at, 0:count] = cosine
        site[1, at, 0:count] = sine
        ch, cl = split(cosine)
        sh, sl = split(sine)
        for ref, cv, sv in ((fwd_hi, ch, sh), (fwd_lo, cl, sl)):
            ref[at, 0:count] = cv
            ref[at, count:2 * count] = -sv
            ref[low, 0:count] = sv
            ref[low, count:2 * count] = cv
        return carry

    lax.fori_loop(0, first_len, build, 0)

    def turn(b, carry):
        at = pl.ds(pl.multiple_of(b * 128, 128), 128)
        low = pl.ds(pl.multiple_of(count + b * 128, 128), 128)
        ch, cl = split(site[0, :, at].T)
        sh, sl = split(site[1, :, at].T)
        for ref, cv, sv in ((inv_hi, ch, sh), (inv_lo, cl, sl)):
            ref[at, 0:count] = cv
            ref[at, count:2 * count] = sv
            ref[low, 0:count] = -sv
            ref[low, count:2 * count] = cv
        return carry

    lax.fori_loop(0, count // 128, turn, 0)

    tiles = width // LANES
    flat = buf.reshape(tiles, count * rows, LANES)
    by_owner = buf.reshape(tiles, n, k_local, rows, LANES)

    def take(start, size):
        return jnp.concatenate([flat[j, pl.ds(start, size, stride=rows), :] for j in range(tiles)], axis=1)

    def put(start, size, value):
        for j in range(tiles):
            flat[j, pl.ds(start, size, stride=rows), :] = value[:, j * LANES:(j + 1) * LANES]

    def lanes_of(j):
        return pl.ds(j * LANES, LANES)


    def chunk_step(c, carry):
        slot = lax.rem(c, 2)
        loads = []
        for j in range(tiles):
            loads.append(pltpu.make_async_copy(
                x_hbm.at[:, pl.ds(row_of(me, c), rows), lanes_of(j)],
                buf.at[j, pl.ds(me * k_local, k_local)], load_sem.at[n - 1, j]))
            loads[-1].start()
        for i in range(len(peers)):
            fwd_copy(c, i).wait_recv()
            at = pl.ds(peers[i] * k_local, k_local)
            for j in range(tiles):
                loads.append(pltpu.make_async_copy(
                    recv_hbm.at[c, at, :, lanes_of(j)], buf.at[j, at], load_sem.at[i, j]))
                loads[-1].start()
        for load in loads:
            load.wait()

        kb = k_local

        def stage(b, carry):
            lane = lax.broadcasted_iota(jnp.int32, (kb, width), 1)
            at = pl.ds(pl.multiple_of(b * kb, kb), kb)
            low = pl.ds(pl.multiple_of(count + b * kb, kb), kb)
            for p in range(pairs):
                r0 = take(b * (kb * rows) + 2 * p, kb)
                r1 = take(b * (kb * rows) + 2 * p + 1, kb)
                re = jnp.where(lane < half, r0, pltpu.roll(r1, half, 1))
                im = jnp.where(lane < half, pltpu.roll(r0, half, 1), r1)
                here = pl.ds(p * width, width)
                rh, rl = split(re)
                ih, il = split(im)
                zhi[at, here] = rh
                zlo[at, here] = rl
                zhi[low, here] = ih
                zlo[low, here] = il
            return carry

        lax.fori_loop(0, count // kb, stage, 0)

        def forward(step, carry):
            m, t = lax.div(step, 3), lax.rem(step, 3)
            plane, part = lax.div(m, 2), lax.rem(m, 2)
            left = pl.ds(pl.multiple_of(m * hr, hr), hr)
            right = pl.ds(pl.multiple_of(t * (cols // 3), cols // 3), cols // 3)
            value = mm3((fwd_hi[left, :], fwd_lo[left, :]), (zhi[:, right], zlo[:, right]))
            site[plane, pl.ds(pl.multiple_of(part * hr, hr), hr), right] = value
            return carry

        lax.fori_loop(0, 12, forward, 0)

        mine = pl.multiple_of(core * hr, hr)
        other = pl.multiple_of((1 - core) * hr, hr)
        gs_copy = pltpu.make_async_remote_copy(
            src_ref=site.at[:, pl.ds(other, hr), :], dst_ref=gs.at[slot],
            send_sem=gs_send, recv_sem=gs_recv.at[slot], device_id=sibling, device_id_type=MESH)
        gs_copy.start()
        gs_copy.wait_recv()

        rb = 16

        def pair(b, carry):
            here = pl.ds(pl.multiple_of(b * rb, rb), rb)
            at = pl.ds(pl.multiple_of(mine + b * rb, rb), rb)
            ore, oim = site[0, at, :], site[1, at, :]
            sre, sim = gs[slot, 0, here, :], gs[slot, 1, here, :]
            qsend[0, here, :] = ore * sre + oim * sim
            qsend[1, here, :] = sgn * (oim * sre - ore * sim)
            return carry

        lax.fori_loop(0, hr // rb, pair, 0)

        q_copy = pltpu.make_async_remote_copy(
            src_ref=qsend, dst_ref=q.at[slot, :, pl.ds(mine, hr), :],
            send_sem=q_send, recv_sem=q_recv.at[slot], device_id=across, device_id_type=MESH)
        q_copy.start()
        q_copy.wait_recv()
        relay = pltpu.make_async_remote_copy(
            src_ref=q.at[slot, :, pl.ds(mine, hr), :], dst_ref=q.at[slot, :, pl.ds(mine, hr), :],
            send_sem=rel_send, recv_sem=rel_recv.at[slot], device_id=sibling, device_id_type=MESH)
        relay.start()

        def sigma_rows(base):
            def body(b, carry):
                at = pl.ds(pl.multiple_of(base + b * rb, rb), rb)
                low = pl.ds(pl.multiple_of(count + base + b * rb, rb), rb)
                gre, gim = site[0, at, :], site[1, at, :]
                qre, qim = q[slot, 0, at, :], sgn * q[slot, 1, at, :]
                rh, rl = split(gim * qim - gre * qre)
                ih, il = split(-(gre * qim + gim * qre))
                zhi[at, :] = rh
                zlo[at, :] = rl
                zhi[low, :] = ih
                zlo[low, :] = il
                return carry

            lax.fori_loop(0, hr // rb, body, 0)

        sigma_rows(mine)
        relay.wait_recv()
        sigma_rows(other)

        def inverse(step, carry):
            m, t = lax.div(step, 2), lax.rem(step, 2)
            top = pl.ds(pl.multiple_of(m * hr, hr), hr)
            bot = pl.ds(pl.multiple_of(count + m * hr, hr), hr)
            right = pl.ds(pl.multiple_of(t * (2 * width), 2 * width), 2 * width)
            z = (zhi[:, right], zlo[:, right])
            re = mm3((inv_hi[top, :], inv_lo[top, :]), z)
            im = mm3((inv_hi[bot, :], inv_lo[bot, :]), z)
            lane = lax.broadcasted_iota(jnp.int32, (hr, width), 1)
            for p in range(2):
                rep = re[:, p * width:(p + 1) * width]
                imp = im[:, p * width:(p + 1) * width]
                r0 = jnp.where(lane < half, rep, pltpu.roll(imp, half, 1))
                r1 = jnp.where(lane < half, pltpu.roll(rep, half, 1), imp)
                base = m * (hr * rows) + t * 4 + 2 * p
                put(base, hr, r0)
                put(base + 1, hr, r1)
            return carry

        lax.fori_loop(0, 4, inverse, 0)

        outs = []
        for j in range(tiles):
            outs.append(pltpu.make_async_copy(buf.at[j], recv_hbm.at[c, :, :, lanes_of(j)], stage_sem.at[j]))
            outs.append(pltpu.make_async_copy(
                buf.at[j, pl.ds(me * k_local, early)],
                sig_hbm.at[:, pl.ds(row_of(me, c), rows), lanes_of(j)], own_sem.at[j]))
            for i, owner in enumerate(peers + [me]):
                outs.append(pltpu.make_async_copy(
                    by_owner.at[j, owner, pl.ds(early, late)],
                    late_hbm[i].at[:, pl.ds(pl.multiple_of(c * rows, rows), rows), lanes_of(j)], late_sem.at[i, j]))
        for out in outs:
            out.start()
        for out in outs:
            out.wait()

        for i in range(len(peers)):
            ret_copy(c, i).start()
        gs_copy.wait_send()
        q_copy.wait_send()
        relay.wait_send()
        return carry

    lax.fori_loop(0, chunks, chunk_step, 0)

    def finish(c, carry):
        for i in range(len(peers)):
            fwd_copy(c, i).wait_send()
            ret_copy(c, i).wait()
        return carry

    lax.fori_loop(0, chunks, finish, 0)


def born_call(n, x, order, first_len):
    k_local, full, width = x.shape
    count = n * k_local
    rows = SUBLANES
    chunks = full // n // rows
    cols = rows * width // 2
    tiles = width // LANES
    hr = count // 2
    late = k_local // LATE_SHARE
    any_spec = pl.BlockSpec(memory_space=pl.ANY)
    vmem = pl.BlockSpec(memory_space=pltpu.VMEM)
    dma = pltpu.SemaphoreType.DMA
    return pl.pallas_call(
        functools.partial(born_kernel, n, chunks, first_len),
        out_shape=(
            jax.ShapeDtypeStruct((chunks, count, rows, width), F32),
            jax.ShapeDtypeStruct((k_local - late, full, width), F32),
            *[jax.ShapeDtypeStruct((late, full // n, width), F32)] * n,
        ),
        in_specs=[any_spec, vmem],
        out_specs=(any_spec,) * (2 + n),
        scratch_shapes=[
            pltpu.VMEM((first_len + count // first_len, count), F32),
            pltpu.VMEM((first_len + count // first_len, count), F32),
            pltpu.VMEM((tiles, count, rows, LANES), F32),
            pltpu.VMEM((2, count, cols), F32),
            pltpu.VMEM((2, 2, hr, cols), F32),
            pltpu.VMEM((2, hr, cols), F32),
            pltpu.VMEM((2, 2, count, cols), F32),
            pltpu.VMEM((2 * count, cols), BF16),
            pltpu.VMEM((2 * count, cols), BF16),
            pltpu.VMEM((2 * count, 2 * count), BF16),
            pltpu.VMEM((2 * count, 2 * count), BF16),
            pltpu.VMEM((2 * count, 2 * count), BF16),
            pltpu.VMEM((2 * count, 2 * count), BF16),
            dma((chunks, n - 1)), dma((chunks, n - 1)), dma((n, tiles)),
            dma(()), dma((2,)), dma(()), dma((2,)), dma(()), dma((2,)),
            dma((chunks, n - 1)), dma((chunks, n - 1)),
            dma((tiles,)), dma((tiles,)), dma((n, tiles)),
        ],
        compiler_params=pltpu.CompilerParams(
            collective_id=0, has_side_effects=True, vmem_limit_bytes=67043328
        ),
        name="born",
    )(x, order)


def on_device(green_guess, green_free, retarded, momentum_order):
    n = lax.axis_size("mom")
    k_local, full, width = green_guess.shape[1:]
    count = n * k_local
    fits = n & (n - 1) == 0 and count & (count - 1) == 0 and full % (n * SUBLANES) == 0 and lax.axis_size("comp") == 4 and count % 512 == 0 and width % LANES == 0 and k_local % LATE_SHARE == 0
    if not fits:
        return on_device_plain(green_guess, green_free, retarded, momentum_order)
    _, sigma, *late = born_call(n, green_guess[0], momentum_order.astype(jnp.int32)[None], L1)
    pieces = send_late(late, n)
    green, sigma = dyson_early(sigma, retarded, green_free[0])
    green, sigma = dyson_late(pieces, retarded, green_free[0], green, sigma)
    return green[None], sigma[None]


def solution(mesh):
    return jax.shard_map(
        on_device,
        mesh=mesh,
        in_specs=(
            P("comp", "mom", None, None),
            P("comp", "mom", None, None),
            P("mom", None, None),
            P(),
        ),
        out_specs=(P("comp", "mom", None, None), P("comp", "mom", None, None)),
        check_vma=False,
    )
```
